32 devices in a mesh: blk: 2 (over y), visit: 4 (over z), patch: 2 (over x), row: 2 (over core).
Axes of the slice: x: 2, y: 2, z: 4, core: 2. Of those that a mesh axis runs over, the one named last changes fastest.
Arguments:
- exposures: bfloat16 [8, 4, 256, 4096], P(('blk', 'visit'), 'patch', 'row'), parts along dimension 0, may hold values from -6 to 6
- kernel_choice: int32 [8, 4], P(('blk', 'visit'), 'patch'), parts along dimension 0, may hold values from 0 to 15
- kernel_coeffs: float32 [9, 16], replicated, may hold values from -2 to 2
- row_taps: bfloat16 [9, 21], replicated, may hold values from -1.25 to 1.25
- column_taps: bfloat16 [9, 21], replicated, may hold values from -1.25 to 1.25
- visit_weight: bfloat16 [8, 4], P('blk'), parts along dimension 0, may hold values from 0.29882812 to 3
- footprints: int32 [3, 8, 2, 32], P(None, 'blk', 'patch'), parts along dimension 1, may hold values from -1 to 3967, as said below
- star_coeffs: float32 [4, 32, 2048], P(('blk', 'patch'), None, ('visit', 'row')), parts along dimension 0, may hold values from -180 to 180
Outputs:
- coadd: float32 [4, 8, 256, 128], P(('blk', 'patch'), 'visit', 'row'), parts along dimension 0
- psf_factor: float32 [4, 32, 32], P(('blk', 'patch')), parts along dimension 0
- whitened: float32 [4, 32, 2048], P(('blk', 'patch'), None, ('visit', 'row')), parts along dimension 0
The draws below stay inside these ranges and needn't reach their ends.
There are 2 independent parts, one for each index of `blk`. The reference program is written for one: setup_inputs(seed, part) draws one part's arguments, and reference() takes and returns one part's arrays. A program takes and returns all parts, laid end to end along the dimension named above; an argument that names none is the same for every part. Nothing has to cross between parts.
Inputs may be any that keep to these rules, and one draw needn't show every extreme that they name: `footprints`: for source visit index s, patch p and entry q: field 0 is the source block k of visit s + k // 2 and CCD p * 2 + k % 2, or -1 for an empty entry; field 1 is the column offset, at most 3967; field 2 the tile slot, 0 to 1. Entry q goes to the owner with visit index q // 8, so at most 8 entries pass from one source to one owner, and in every patch one owner receives 8 live entries from every source. Every tile slot of every owner receives at least one live entry. Empty entries hold 0 in fields 1 and 2.
All inputs are finite; a program needn't handle non-finite values.
Results may differ from the reference program's by a relative error of at most 0.007.
Values may be sent and summed in bfloat16 or wider, within the bound.
A program may use at most 192 MiB of HBM per device.

```python
import math
from functools import partial
import jax
import jax.numpy as jnp
from jax import lax

TAPS = 21
NBASIS = 9
NCOEF = 16
NCOMP = 32
V_DEV = 1
C_DEV = 2
CW = 4096
TW = 128
CAP = 8
TILES_DEV = 2
HALF = 10
SOURCES = 4
PATCHES = 2
VISITS = 4
CCDS = 4
CROWS = 256
SLABS = 2
SLOTS = 32
TILES = 8
STARS = 2048


def draw_footprints(key, part):
    subkeys = jax.random.split(key, 5)
    full_shape = (SOURCES, PATCHES, SLOTS)
    busiest = jax.random.randint(subkeys[0], (1, PATCHES, 1), 0, SOURCES)
    source = jnp.arange(SOURCES, dtype=jnp.int32)[:, None, None]
    target = (jnp.arange(SLOTS, dtype=jnp.int32) // CAP)[None, None, :]
    lane_index = (jnp.arange(SLOTS, dtype=jnp.int32) % CAP)[None, None, :]
    covering = jnp.broadcast_to(source == (target + 1) % SOURCES, full_shape)
    chosen = jax.random.randint(subkeys[1], full_shape, 0, 3) == 0
    hole = (source == busiest) & (target == (busiest + 2) % SOURCES) & (lane_index == CAP - 1)
    live_mask = ((target == busiest) | covering | chosen) & jnp.logical_not(hole)
    corner = (source == 0) & (target == busiest) & (lane_index == 0)
    slab_ids = jnp.where(corner, SLABS - 1, jax.random.randint(subkeys[2], full_shape, 0, SLABS))
    offsets = jnp.where(corner, CW - TW - 1, jax.random.randint(subkeys[3], full_shape, 0, CW - TW))
    slot_ids = jnp.where(covering, jnp.broadcast_to(lane_index % TILES_DEV, full_shape), jax.random.randint(subkeys[4], full_shape, 0, TILES_DEV))
    slab_ids = jnp.where(live_mask, slab_ids, -1)
    offsets = jnp.where(live_mask, offsets, 0)
    slot_ids = jnp.where(live_mask, slot_ids, 0)
    return jnp.stack([slab_ids, offsets, slot_ids]).astype(jnp.int32)


def draw_star_coeffs(key, part):
    subkeys = jax.random.split(key, 3)
    position = jnp.arange(STARS, dtype=jnp.float32) / STARS
    row_scale = jnp.exp(jnp.log(10.0) * jax.random.uniform(subkeys[1], (PATCHES, 1, STARS))) * jnp.power(3.0, position)
    column_scale = jnp.exp(jnp.log(10.0) * jax.random.uniform(subkeys[2], (PATCHES, NCOMP, 1)))
    entries = jnp.clip(jax.random.normal(subkeys[0], (PATCHES, NCOMP, STARS)), -6.0, 6.0)
    return (0.1 * entries * row_scale * column_scale).astype(jnp.float32)


def touch_ends(values, rng, smallest, largest):
    longest = values.shape.index(max(values.shape))
    spots = []
    for shift in (0, 1):
        where = [jax.random.randint(jax.random.fold_in(rng, axis), (), 0, length) for axis, length in enumerate(values.shape)]
        where[longest] = (where[longest] + shift) % values.shape[longest]
        spots.append(tuple(where))
    return values.at[spots[0]].set(smallest).at[spots[1]].set(largest)


def block_scale(stream_key, shape, pieces, least, high):
    loudness = 1.0
    for dim, blocks in pieces:
        steps = jax.random.uniform(jax.random.fold_in(jax.random.fold_in(stream_key, 6), dim), (blocks,), jnp.float32, least / len(pieces), high / len(pieces))
        loudness = loudness * jnp.repeat(jnp.exp(steps), shape[dim] // blocks).reshape((-1,) + (1,) * (len(shape) - 1 - dim))
    return loudness


def noise(stream_key, shape, scale, most, cuts=(), held_as=jnp.bfloat16):
    array = scale * jax.random.normal(stream_key, shape, jnp.float32)
    if cuts:
        array = array * block_scale(stream_key, shape, cuts, -0.22, 0.18)
    return jnp.clip(array, -most, most).astype(held_as)


def setup_inputs(seed: int = 0, part: int = 0) -> dict:
    key_of = jax.random.split(jax.random.key(seed), 9)
    own_keys = jax.random.split(jax.random.fold_in(key_of[8], part), 9)
    return {
        "exposures": noise(own_keys[0], (VISITS, CCDS, CROWS, CW), 1.0, 6.0, ((0, 4), (1, 2), (2, 2))),
        "kernel_choice": touch_ends(jax.random.randint(own_keys[1], (VISITS, CCDS), 0, NCOEF), jax.random.fold_in(own_keys[1], 1), 0, NCOEF - 1).astype(jnp.int32),
        "kernel_coeffs": noise(key_of[2], (NBASIS, NCOEF), NBASIS ** -0.5, 2.0, (), jnp.float32),
        "row_taps": noise(key_of[3], (NBASIS, TAPS), TAPS ** -0.5, 1.25),
        "column_taps": noise(key_of[4], (NBASIS, TAPS), TAPS ** -0.5, 1.25),
        "visit_weight": jnp.clip(jnp.exp(jax.random.uniform(own_keys[5], (VISITS, CCDS), jnp.float32, math.log(0.29882812), math.log(3.0))), 0.29882812, 3.0).astype(jnp.bfloat16),
        "footprints": draw_footprints(jax.random.fold_in(jax.random.fold_in(key_of[8], part), 71), part),
        "star_coeffs": draw_star_coeffs(jax.random.fold_in(jax.random.fold_in(key_of[8], part), 71), part),
    }


HIGHEST = lax.Precision.HIGHEST
BILINEAR = (0.28125, 0.46875, 0.09375, 0.15625)

def match_image(operands, column_taps):
    image, mixing = operands
    padded = jnp.pad(image.astype(jnp.float32), ((0, 0), (HALF, HALF)))
    shifted = jnp.stack([padded[:, offset:offset + CW] for offset in range(TAPS)])
    filtered = jnp.einsum('bt,trc->brc', column_taps.astype(jnp.float32), shifted, precision=HIGHEST).astype(jnp.bfloat16)
    padded_rows = jnp.pad(filtered.astype(jnp.float32), ((0, 0), (HALF, HALF), (0, 0)))
    stacked = jnp.stack([padded_rows[:, offset:offset + CROWS, :] for offset in range(TAPS)], axis=1)
    summed = jnp.einsum('bt,btrc->rc', mixing.astype(jnp.float32), stacked, precision=HIGHEST)
    return summed.astype(jnp.bfloat16)

def reference(exposures, kernel_choice, kernel_coeffs, row_taps, column_taps, visit_weight, footprints, star_coeffs):
    gram = jnp.einsum('pks,pls->pkl', star_coeffs, star_coeffs, precision=HIGHEST)
    psf_factor = jnp.linalg.cholesky(gram) / math.sqrt(STARS)
    whitened = lax.linalg.triangular_solve(psf_factor, star_coeffs, left_side=True, lower=True)
    factor_diag = jnp.diagonal(psf_factor, axis1=1, axis2=2)[:, :NBASIS]
    basis_scale = factor_diag / jnp.sqrt(lax.optimization_barrier(jnp.mean(factor_diag * factor_diag, axis=1, keepdims=True)))
    ccd_scale = jnp.repeat(basis_scale, C_DEV, axis=0)
    coefficient = jnp.transpose(kernel_coeffs)[kernel_choice] * ccd_scale[None]
    mixing = (coefficient[..., None] * row_taps.astype(jnp.float32)).astype(jnp.bfloat16)
    images = exposures.reshape(VISITS * CCDS, CROWS, CW)
    mixes = mixing.reshape(VISITS * CCDS, NBASIS, TAPS)
    matched = lax.map(partial(match_image, column_taps=column_taps), (images, mixes))
    matched = jnp.pad(matched.reshape(VISITS, CCDS, CROWS, CW), ((0, 0), (0, 0), (0, 1), (0, 0)))
    patch_ids = jnp.arange(PATCHES, dtype=jnp.int32)[:, None]
    tile_ids = jnp.arange(TILES, dtype=jnp.int32)
    target_base = jnp.arange(SLOTS, dtype=jnp.int32) // CAP * TILES_DEV

    def cut_window(visit_id, ccd_id, offset):
        return lax.dynamic_slice(matched, (visit_id, ccd_id, jnp.int32(0), offset), (1, 1, CROWS + 1, TW + 1))[0, 0]

    def add_source(carry, source):
        numerator, totals = carry
        fields = lax.dynamic_index_in_dim(footprints, source, axis=1, keepdims=False)
        slab_ids = fields[0]
        safe_ids = jnp.maximum(slab_ids, 0)
        visit_ids = (source * V_DEV + safe_ids // C_DEV).astype(jnp.int32)
        ccd_ids = (patch_ids * C_DEV + safe_ids % C_DEV).astype(jnp.int32)
        windows = jax.vmap(jax.vmap(cut_window))(visit_ids, ccd_ids, fields[1].astype(jnp.int32)).astype(jnp.float32)
        warped = (BILINEAR[0] * windows[:, :, :-1, :-1] + BILINEAR[1] * windows[:, :, :-1, 1:] + BILINEAR[2] * windows[:, :, 1:, :-1] + BILINEAR[3] * windows[:, :, 1:, 1:]).astype(jnp.bfloat16)
        weights = jnp.where(slab_ids >= 0, visit_weight[visit_ids, ccd_ids].astype(jnp.float32), 0.0)
        targets = target_base[None, :] + fields[2]
        spread = jnp.where(targets[:, :, None] == tile_ids, weights[:, :, None], 0.0)
        contribution = jnp.einsum('pqg,pqrc->pgrc', spread, warped.astype(jnp.float32), precision=HIGHEST)
        contribution = lax.optimization_barrier(contribution.astype(jnp.bfloat16)).astype(jnp.float32)
        numerator = numerator + contribution
        totals = totals + lax.optimization_barrier(jnp.sum(spread, axis=1))
        return ((numerator, totals), None)
    start = (jnp.zeros((PATCHES, TILES, CROWS, TW), jnp.float32), jnp.zeros((PATCHES, TILES), jnp.float32))
    (numerator, totals), unused = lax.scan(add_source, start, jnp.arange(SOURCES, dtype=jnp.int32))
    coadd = numerator / totals[:, :, None, None]
    return (coadd, psf_factor, whitened)
```

```python
import functools
import math

import jax
import jax.numpy as jnp
from jax import lax
from jax.experimental import pallas as pl
from jax.experimental.pallas import tpu as pltpu
from jax.sharding import PartitionSpec as P

NBASIS = 9
NTAPS = 21
C_DEV = 2
R_DEV = 128
CW = 4096
TW = 128
CAP = 8
TILES_DEV = 2
HALF = 10
SLABS = 2
HALO = 16
ROWS = R_DEV + HALO
NCOMP = 32
PAD = 128
PLACES = TILES_DEV * SLABS
PAIRS = SLABS * NBASIS
OWN_K = PAIRS * R_DEV
HALO_TILES = 3
ALL_K = OWN_K + HALO_TILES * TW
UNIT = 32
OWNERS_UNROLLED = 4
HIGHEST = lax.Precision.HIGHEST
VMEM_LIMIT = 48 * 1024 * 1024
MESH = pl.DeviceIdType.MESH


def iota(shape, axis):
    return lax.broadcasted_iota(jnp.int32, shape, axis)


def factor_steps(gram, stars):
    sub = iota((NCOMP, 1), 0)
    lane = iota((NCOMP, NCOMP), 1)
    lower = jnp.zeros((NCOMP, NCOMP), jnp.float32)
    for j in range(NCOMP):
        inv = 1.0 / jnp.sqrt(gram[j : j + 1, j : j + 1])
        column = gram[:, j : j + 1] * inv
        lower = jnp.where((lane == j) & (sub >= j), column, lower)
        below = jnp.where(sub > j, column, 0.0)
        solved = stars[j : j + 1, :] * inv
        gram = gram - below * (gram[j : j + 1, :] * inv)
        stars = jnp.where(sub == j, solved, stars - below * solved)
    return lower, stars


def pack(square):
    return jnp.concatenate([square[a : a + 8] for a in range(0, NCOMP, 8)], axis=1)


def unpack(packed):
    return jnp.concatenate([packed[:, a : a + NCOMP] for a in range(0, TW, NCOMP)], axis=0)


def basis_scales(packed):
    full = (8, TW)
    columns = [jnp.broadcast_to(packed[:, j : j + 1], full) for j in range(8)]
    ninth = [jnp.broadcast_to(packed[0:1, NCOMP + j : NCOMP + j + 1], full) for j in range(NBASIS)]
    pivots = []
    for j in range(8):
        pivot = jnp.broadcast_to(columns[j][j : j + 1], full)
        pivots.append(pivot)
        inverse = 1.0 / pivot
        for k in range(j + 1, 8):
            ratio = jnp.broadcast_to(columns[j][k : k + 1], full) * inverse
            columns[k] = columns[k] - columns[j] * ratio
            ninth[k] = ninth[k] - ninth[j] * ratio
        ninth[8] = ninth[8] - ninth[j] * (ninth[j] * inverse)
    pivots.append(ninth[8])
    total = pivots[0]
    for pivot in pivots[1:]:
        total = total + pivot
    norm = 1.0 / jnp.sqrt(total / NBASIS)
    return [jnp.sqrt(pivot) * norm for pivot in pivots]


def choose(entries, unit):
    shape = (PLACES * unit, CAP * unit)
    sub, lane = iota(shape, 0), iota(shape, 1)
    spot = iota((1, CAP * unit), 1)
    place = jnp.full(spot.shape, -1, jnp.int32)
    for e, entry in enumerate(entries):
        place = jnp.where(spot >= e * unit, entry[0], place)
    bits = unit.bit_length() - 1
    same = jnp.bitwise_and(sub, unit - 1) == jnp.bitwise_and(lane, unit - 1)
    hit = same & (lax.shift_right_logical(sub, bits) == place)
    return jnp.where(hit, 1.0, 0.0).astype(jnp.bfloat16)


def coadd_kernel(
    visits,
    rows_count,
    star_total,
    choice_hbm,
    list_hbm,
    weight_hbm,
    coeff_hbm,
    row_tap_hbm,
    column_tap_hbm,
    star_hbm,
    image_hbm,
    coadd_ref,
    factor_ref,
    white_ref,
    choice_ref,
    list_ref,
    list_vec,
    weight_ref,
    coeff_ref,
    row_tap_ref,
    column_tap_ref,
    star_ref,
    padded,
    sums,
    band,
    z,
    plain,
    mixed,
    grams,
    outgoing,
    incoming,
    small_sem,
    star_sem,
    image_sem,
    halo_send,
    halo_recv,
    gram_send,
    gram_recv,
    tile_send,
    tile_recv,
):
    visit = lax.axis_index("visit")
    row = lax.axis_index("row")
    patch = lax.axis_index("patch")
    members = visits * rows_count
    me = visit * rows_count + row

    def member(step):
        other = lax.rem(me + step, members)
        return {"visit": lax.div(other, rows_count), "row": lax.rem(other, rows_count)}

    barrier = pltpu.get_barrier_semaphore()
    for step in range(1, members):
        pl.semaphore_signal(barrier, inc=1, device_id=member(step), device_id_type=MESH)
    star_copy = pltpu.make_async_copy(star_hbm, star_ref, star_sem)
    star_copy.start()
    small = []
    for source, target in (
        (column_tap_hbm, column_tap_ref),
        (row_tap_hbm, row_tap_ref),
        (coeff_hbm, coeff_ref),
        (weight_hbm, weight_ref),
        (list_hbm, list_vec),
        (choice_hbm, choice_ref),
        (list_hbm, list_ref),
    ):
        copy = pltpu.make_async_copy(source, target, small_sem.at[len(small)])
        copy.start()
        small.append(copy)
    loads = []
    for k in range(SLABS):
        copy = pltpu.make_async_copy(
            image_hbm.at[0, k], padded.at[k, 0:R_DEV, PAD : PAD + CW], image_sem.at[k]
        )
        copy.start()
        loads.append(copy)

    star_copy.wait()
    stars = star_ref[0]
    grams[me] = pack(
        lax.dot_general(
            stars,
            stars,
            (((1,), (1,)), ((), ())),
            precision=HIGHEST,
            preferred_element_type=jnp.float32,
        )
    )
    pl.semaphore_wait(barrier, members - 1)
    gram_copies = []
    for step in range(1, members):
        copy = pltpu.make_async_remote_copy(
            src_ref=grams.at[me],
            dst_ref=grams.at[me],
            send_sem=gram_send.at[step],
            recv_sem=gram_recv.at[step],
            device_id=member(step),
            device_id_type=MESH,
        )
        copy.start()
        gram_copies.append(copy)
    edge = pl.multiple_of((1 - row) * (R_DEV - HALO), HALO)
    halo_copies = []
    for k in range(SLABS):
        copy = pltpu.make_async_remote_copy(
            src_ref=image_hbm.at[0, k, pl.ds(edge, HALO), :],
            dst_ref=padded.at[k, R_DEV:ROWS, PAD : PAD + CW],
            send_sem=halo_send.at[k],
            recv_sem=halo_recv.at[k],
            device_id={"row": 1 - row},
            device_id_type=MESH,
        )
        copy.start()
        halo_copies.append(copy)

    for k in range(SLABS):
        padded[k, :, 0:PAD] = jnp.zeros((ROWS, PAD), jnp.bfloat16)
        padded[k, :, PAD + CW :] = jnp.zeros((ROWS, PAD), jnp.bfloat16)
    rest = ALL_K - OWN_K - PAIRS * HALO
    for copy in small:
        copy.wait()
    tap = iota((NTAPS, 2 * TW), 0)
    lanes = iota((NTAPS, 2 * TW), 1)

    def hits(index):
        return (lanes == jnp.bitwise_and(index, 2 * TW - 1)).astype(jnp.float32)

    reversed_taps = jnp.dot(
        column_tap_ref[...].astype(jnp.float32),
        0.375 * hits(-tap) + 0.625 * hits(-1 - tap),
        precision=HIGHEST,
    )
    for b in range(NBASIS):
        base = jnp.broadcast_to(reversed_taps[b : b + 1, :], (2 * TW, 2 * TW))
        rolled = pltpu.roll(base, 0, 1, stride=1, stride_axis=0)
        band[:, b * TW : (b + 1) * TW] = rolled[:, 0:TW].astype(jnp.bfloat16)

    table = weight_ref[...].astype(jnp.float32)
    cell_visit, cell_ccd = iota(table.shape, 0), iota(table.shape, 1)

    def weight_of(source, k):
        hit = (cell_visit == source) & (cell_ccd == patch * C_DEV + k)
        return jnp.sum(jnp.where(hit, table, 0.0), keepdims=True)

    sets = iota(coeff_ref.shape, 1)
    near, far = hits(tap - HALF), hits(tap + 1 - HALF)
    lane = iota((R_DEV, TW), 1)
    wide_sub = iota((R_DEV, 2 * TW), 0)
    last = (wide_sub == R_DEV - 1) & (row == rows_count - 1)
    halo_parts = [jnp.zeros((R_DEV, TW), jnp.float32) for _ in range(HALO_TILES)]
    for k in range(SLABS):
        picked = jnp.sum(
            jnp.where(sets == choice_ref[0, k], coeff_ref[...], 0.0), axis=1, keepdims=True
        )
        taps = picked * row_tap_ref[...].astype(jnp.float32)
        weight = weight_of(visit, k)
        first = jnp.dot(taps, near, precision=HIGHEST) * (0.75 * weight)
        second = jnp.dot(taps, far, precision=HIGHEST) * (0.25 * weight)
        for b in range(NBASIS):
            m = k * NBASIS + b
            one = jnp.broadcast_to(first[b : b + 1], (R_DEV, 2 * TW))
            two = jnp.broadcast_to(second[b : b + 1], (R_DEV, 2 * TW))
            base = one + jnp.where(last, 0.0, two)
            rolled = pltpu.roll(base, 0, 1, stride=1, stride_axis=0)
            plain[:, m * TW : (m + 1) * TW] = rolled[:, 0:TW]
            low = m % 8 * HALO
            piece = pltpu.roll(rolled[:, TW:], jnp.bitwise_and(low + row * HALO, TW - 1), 1)
            inside = (lane >= low) & (lane < low + HALO)
            halo_parts[m // 8] = jnp.where(inside, piece, halo_parts[m // 8])
    for t in range(HALO_TILES):
        plain[:, OWN_K + t * TW : OWN_K + (t + 1) * TW] = halo_parts[t]

    def add_windows(owner):
        entries = []
        for e in range(CAP):
            q = owner * CAP + e
            k = list_ref[0, visit, 0, q]
            start = list_ref[1, visit, 0, q] + (PAD - HALF)
            tile = lax.shift_right_logical(start, 7)
            shift = start - tile * TW
            place = jnp.where(k >= 0, list_ref[2, visit, 0, q] * SLABS + k, -1)
            back = jnp.bitwise_and(TW - shift, TW - 1)
            entries.append((place, jnp.maximum(k, 0), tile, shift, back))
        for first_row, unit in [(r, UNIT) for r in range(0, R_DEV, UNIT)] + [(R_DEV, HALO)]:
            spot = iota((unit, TW), 1)
            left, right = [], []
            for _, k, tile, shift, back in entries:
                parts = []
                for t in range(3):
                    at = (tile + t) * TW
                    piece = padded[k, first_row : first_row + unit, pl.ds(at, TW)]
                    parts.append(pltpu.roll(piece, back, 1))
                keep = spot < TW - shift
                left.append(jnp.where(keep, parts[0], parts[1]))
                right.append(jnp.where(keep, parts[1], parts[2]))
            windows = jnp.concatenate(
                [jnp.concatenate(left, axis=0), jnp.concatenate(right, axis=0)], axis=1
            )
            out = jnp.dot(choose(entries, unit), windows, preferred_element_type=jnp.float32)
            out = out.astype(jnp.bfloat16)
            for p in range(PLACES):
                sums[owner, p, first_row : first_row + unit, :] = out[p * unit : (p + 1) * unit]

    def filter_columns(owner):
        block = sums[owner].reshape(PLACES * ROWS, 2 * TW)
        out = jnp.dot(block, band[...], preferred_element_type=jnp.float32).astype(jnp.bfloat16)
        for p in range(PLACES):
            slot, k = p // SLABS, p % SLABS
            at = slice(slot * TW, (slot + 1) * TW)
            for b in range(NBASIS):
                m = k * NBASIS + b
                part = out[p * ROWS : (p + 1) * ROWS, b * TW : (b + 1) * TW]
                z[owner, m * R_DEV : (m + 1) * R_DEV, at] = part[:R_DEV]
                halo_at = OWN_K + m * HALO
                z[owner, halo_at : halo_at + HALO, at] = part[R_DEV:]
        z[owner, ALL_K - rest :, :] = jnp.zeros((rest, TILES_DEV * TW), jnp.bfloat16)

    for copy in loads:
        copy.wait()
    for copy in halo_copies:
        copy.wait_recv()

    def prepare(group):
        for o in range(OWNERS_UNROLLED):
            owner = group * OWNERS_UNROLLED + o
            add_windows(owner)
            filter_columns(owner)

    if visits <= OWNERS_UNROLLED:
        for owner in range(visits):
            add_windows(owner)
            filter_columns(owner)
    else:
        pl.loop(0, visits // OWNERS_UNROLLED)(prepare)

    for copy in gram_copies:
        copy.wait_recv()
    packed = grams[0]
    for s in range(1, members):
        packed = packed + grams[s]
    scales = basis_scales(packed)
    for b in range(NBASIS):
        wide = jnp.broadcast_to(scales[b][0:1], (R_DEV, TW))
        for k in range(SLABS):
            at = slice((k * NBASIS + b) * TW, (k * NBASIS + b + 1) * TW)
            mixed[:, at] = (plain[:, at] * wide).astype(jnp.bfloat16)
    spot = iota((8, TW), 1)
    for t in range(HALO_TILES):
        wide = jnp.zeros((8, TW), jnp.float32)
        for m in range(t * 8, min(t * 8 + 8, PAIRS)):
            wide = jnp.where(spot >= m % 8 * HALO, scales[m % NBASIS], wide)
        at = slice(OWN_K + t * TW, OWN_K + (t + 1) * TW)
        wide = jnp.broadcast_to(wide[0:1], (R_DEV, TW))
        mixed[:, at] = (plain[:, at] * wide).astype(jnp.bfloat16)

    def mix_rows(owner):
        out = jnp.dot(mixed[...], z[owner], preferred_element_type=jnp.float32)
        out = out.astype(jnp.bfloat16)
        for g in range(TILES_DEV):
            outgoing[owner, g] = out[:, g * TW : (g + 1) * TW]

    tile_copies = []
    for step in range(visits - 1):
        owner = step + lax.div(step + visits - visit, visits)
        mix_rows(owner)
        copy = pltpu.make_async_remote_copy(
            src_ref=outgoing.at[owner],
            dst_ref=incoming.at[visit],
            send_sem=tile_send.at[step],
            recv_sem=tile_recv.at[visit],
            device_id={"visit": owner},
            device_id_type=MESH,
        )
        copy.start()
        tile_copies.append(copy)
    mix_rows(visit)

    lower, solved = factor_steps(unpack(packed), stars)
    root = math.sqrt(star_total)
    factor_ref[0] = lower / root
    white_ref[0] = solved * root

    slot_lane = iota((1, list_vec.shape[3]), 1)
    mine = (slot_lane >= visit * CAP) & (slot_lane < visit * CAP + CAP)
    totals = [jnp.zeros((1, 1), jnp.float32) for _ in range(TILES_DEV)]
    for s in range(visits):
        block, slot = list_vec[0, s], list_vec[2, s]
        for g in range(TILES_DEV):
            for k in range(SLABS):
                ones = jnp.where(mine & (block == k) & (slot == g), 1.0, 0.0)
                count = jnp.sum(ones, axis=1, keepdims=True)
                totals[g] = totals[g] + count * weight_of(s, k)
    numerators = [outgoing[visit, g].astype(jnp.float32) for g in range(TILES_DEV)]
    for step in range(1, visits):
        source = lax.rem(visit + step, visits)
        pltpu.make_async_remote_copy(
            src_ref=outgoing.at[source],
            dst_ref=incoming.at[source],
            send_sem=tile_send.at[step - 1],
            recv_sem=tile_recv.at[source],
            device_id={"visit": source},
            device_id_type=MESH,
        ).wait_recv()
        for g in range(TILES_DEV):
            numerators[g] = numerators[g] + incoming[source, g].astype(jnp.float32)
    for g in range(TILES_DEV):
        coadd_ref[0, g] = numerators[g] / totals[g]
    for copy in halo_copies + gram_copies + tile_copies:
        copy.wait_send()


def result_kernel(*refs):
    sources, targets, sem = refs[:3], refs[3:6], refs[6]
    copies = []
    for i, (source, target) in enumerate(zip(sources, targets)):
        copy = pltpu.make_async_copy(source, target, sem.at[i])
        copy.start()
        copies.append(copy)
    for copy in copies:
        copy.wait()


def on_device(
    exposures,
    kernel_choice,
    kernel_coeffs,
    row_taps,
    column_taps,
    visit_weight,
    footprints,
    star_coeffs,
):
    visits = lax.axis_size("visit")
    rows_count = lax.axis_size("row")
    members = visits * rows_count
    star_total = star_coeffs.shape[2] * members
    vmem = pl.BlockSpec(memory_space=pltpu.VMEM)
    anywhere = pl.BlockSpec(memory_space=pl.ANY)
    hbm = pl.BlockSpec(memory_space=pltpu.HBM)
    tiles = pltpu.VMEM((visits, TILES_DEV, R_DEV, TW), jnp.bfloat16)
    dma = pltpu.SemaphoreType.DMA
    operands = (
        kernel_choice,
        footprints,
        visit_weight,
        kernel_coeffs,
        row_taps,
        column_taps,
        star_coeffs,
        exposures,
    )
    results = pl.pallas_call(
        functools.partial(coadd_kernel, visits, rows_count, star_total),
        out_shape=(
            jax.ShapeDtypeStruct((1, TILES_DEV, R_DEV, TW), jnp.float32),
            jax.ShapeDtypeStruct((1, NCOMP, NCOMP), jnp.float32),
            jax.ShapeDtypeStruct(star_coeffs.shape, jnp.float32),
        ),
        in_specs=[hbm] * 8,
        out_specs=(vmem, vmem, vmem),
        scratch_shapes=[
            pltpu.SMEM(kernel_choice.shape, jnp.int32),
            pltpu.SMEM(footprints.shape, jnp.int32),
            pltpu.VMEM(footprints.shape, jnp.int32),
            pltpu.VMEM(visit_weight.shape, jnp.bfloat16),
            pltpu.VMEM(kernel_coeffs.shape, jnp.float32),
            pltpu.VMEM(row_taps.shape, jnp.bfloat16),
            pltpu.VMEM(column_taps.shape, jnp.bfloat16),
            pltpu.VMEM(star_coeffs.shape, jnp.float32),
            pltpu.VMEM((SLABS, ROWS, CW + 2 * PAD), jnp.bfloat16),
            pltpu.VMEM((visits, PLACES, ROWS, 2 * TW), jnp.bfloat16),
            pltpu.VMEM((2 * TW, NBASIS * TW), jnp.bfloat16),
            pltpu.VMEM((visits, ALL_K, TILES_DEV * TW), jnp.bfloat16),
            pltpu.VMEM((R_DEV, ALL_K), jnp.float32),
            pltpu.VMEM((R_DEV, ALL_K), jnp.bfloat16),
            pltpu.VMEM((members, 8, TW), jnp.float32),
            tiles,
            tiles,
            dma((7,)),
            dma,
            dma((SLABS,)),
            dma((SLABS,)),
            dma((SLABS,)),
            dma((members,)),
            dma((members,)),
            dma((visits,)),
            dma((visits,)),
        ],
        compiler_params=pltpu.CompilerParams(
            vmem_limit_bytes=VMEM_LIMIT, collective_id=0, has_side_effects=True
        ),
        name="coadd",
    )(*[pltpu.with_memory_space_constraint(x, pltpu.HBM) for x in operands])
    return pl.pallas_call(
        result_kernel,
        out_shape=tuple(jax.ShapeDtypeStruct(part.shape, part.dtype) for part in results),
        in_specs=[anywhere] * 3,
        out_specs=(anywhere,) * 3,
        scratch_shapes=[dma((3,))],
        compiler_params=pltpu.CompilerParams(vmem_limit_bytes=4 * 1024 * 1024),
        name="results",
    )(*results)


def solution(mesh):
    in_specs = (
        P(("blk", "visit"), "patch", "row", None),
        P(("blk", "visit"), "patch"),
        P(),
        P(),
        P(),
        P("blk", None),
        P(None, "blk", "patch", None),
        P(("blk", "patch"), None, ("visit", "row")),
    )
    out_specs = (
        P(("blk", "patch"), "visit", "row", None),
        P(("blk", "patch"), None, None),
        P(("blk", "patch"), None, ("visit", "row")),
    )
    return jax.shard_map(
        on_device, mesh=mesh, in_specs=in_specs, out_specs=out_specs, check_vma=False
    )
```

```python
import functools
import math

import jax
import jax.numpy as jnp
from jax import lax
from jax.experimental import pallas as pl
from jax.experimental.pallas import tpu as pltpu
from jax.sharding import PartitionSpec as P

NBASIS = 9
NTAPS = 21
C_DEV = 2
R_DEV = 128
CW = 4096
TW = 128
CAP = 8
TILES_DEV = 2
HALF = 10
SLABS = 2
HALO = 16
ROWS = R_DEV + HALO
NCOMP = 32
PAD = 128
PLACES = TILES_DEV * SLABS
PAIRS = SLABS * NBASIS
OWN_K = PAIRS * R_DEV
HALO_K = 2 * TW
ALL_K = OWN_K + SLABS * HALO_K
BEFORE = 2
UNIT = 32
HIGHEST = lax.Precision.HIGHEST
VMEM_LIMIT = 48 * 1024 * 1024
MESH = pl.DeviceIdType.MESH


def iota(shape, axis):
    return lax.broadcasted_iota(jnp.int32, shape, axis)


def factor_steps(gram, stars):
    sub = iota((NCOMP, 1), 0)
    lane = iota((NCOMP, NCOMP), 1)
    lower = jnp.zeros((NCOMP, NCOMP), jnp.float32)
    for j in range(NCOMP):
        inv = 1.0 / jnp.sqrt(gram[j : j + 1, j : j + 1])
        column = gram[:, j : j + 1] * inv
        lower = jnp.where((lane == j) & (sub >= j), column, lower)
        below = jnp.where(sub > j, column, 0.0)
        solved = stars[j : j + 1, :] * inv
        gram = gram - below * (gram[j : j + 1, :] * inv)
        stars = jnp.where(sub == j, solved, stars - below * solved)
    return lower, stars


def pack(square):
    return jnp.concatenate([square[a : a + 8] for a in range(0, NCOMP, 8)], axis=1)


def unpack(packed):
    return jnp.concatenate([packed[:, a : a + NCOMP] for a in range(0, TW, NCOMP)], axis=0)


def basis_scales(packed):
    full = (8, TW)
    columns = [jnp.broadcast_to(packed[:, j : j + 1], full) for j in range(8)]
    ninth = [jnp.broadcast_to(packed[0:1, NCOMP + j : NCOMP + j + 1], full) for j in range(NBASIS)]
    pivots = []
    for j in range(8):
        pivot = jnp.broadcast_to(columns[j][j : j + 1], full)
        pivots.append(pivot)
        inverse = 1.0 / pivot
        for k in range(j + 1, 8):
            ratio = jnp.broadcast_to(columns[j][k : k + 1], full) * inverse
            columns[k] = columns[k] - columns[j] * ratio
            ninth[k] = ninth[k] - ninth[j] * ratio
        ninth[8] = ninth[8] - ninth[j] * (ninth[j] * inverse)
    pivots.append(ninth[8])
    total = pivots[0]
    for pivot in pivots[1:]:
        total = total + pivot
    norm = 1.0 / jnp.sqrt(total / NBASIS)
    return [jnp.sqrt(pivot) * norm for pivot in pivots]


def choose(entries, unit):
    shape = (PLACES * unit, CAP * unit)
    sub, lane = iota(shape, 0), iota(shape, 1)
    spot = iota((1, CAP * unit), 1)
    place = jnp.full(spot.shape, -1, jnp.int32)
    for e, entry in enumerate(entries):
        place = jnp.where(spot >= e * unit, entry[0], place)
    bits = unit.bit_length() - 1
    same = jnp.bitwise_and(sub, unit - 1) == jnp.bitwise_and(lane, unit - 1)
    hit = same & (lax.shift_right_logical(sub, bits) == place)
    return jnp.where(hit, 1.0, 0.0).astype(jnp.bfloat16)


def coadd_kernel(
    visits,
    rows_count,
    star_total,
    choice_hbm,
    list_hbm,
    weight_hbm,
    coeff_hbm,
    row_tap_hbm,
    column_tap_hbm,
    star_hbm,
    image_hbm,
    coadd_ref,
    factor_ref,
    white_ref,
    choice_ref,
    list_ref,
    list_vec,
    weight_ref,
    coeff_ref,
    row_tap_ref,
    column_tap_ref,
    star_ref,
    padded,
    sums,
    band,
    z,
    plain,
    chosen,
    mixed,
    grams,
    pair_sum,
    outgoing,
    incoming,
    small_sem,
    star_sem,
    image_sem,
    halo_send,
    halo_recv,
    gram_send,
    gram_recv,
    up_send,
    ready,
    tile_send,
    tile_recv,
):
    visit = lax.axis_index("visit")
    row = lax.axis_index("row")
    patch = lax.axis_index("patch")
    members = visits * rows_count
    me = visit * rows_count + row
    lower_count = visit * rows_count

    def at(other_visit, other_row):
        return {"visit": other_visit, "row": other_row}

    barrier = pltpu.get_barrier_semaphore()
    pl.semaphore_signal(barrier, inc=1, device_id=at(visit, 1 - row), device_id_type=MESH)
    for step in range(visits - 1, 0, -1):

        @pl.when(visit + step < visits)
        def _():
            for r in range(rows_count):
                pl.semaphore_signal(barrier, inc=1, device_id=at(visit + step, r), device_id_type=MESH)

    star_copy = pltpu.make_async_copy(star_hbm, star_ref, star_sem)
    star_copy.start()
    small = []
    for source, target in (
        (column_tap_hbm, column_tap_ref),
        (row_tap_hbm, row_tap_ref),
        (coeff_hbm, coeff_ref),
        (weight_hbm, weight_ref),
        (list_hbm, list_vec),
        (choice_hbm, choice_ref),
        (list_hbm, list_ref),
    ):
        copy = pltpu.make_async_copy(source, target, small_sem.at[len(small)])
        copy.start()
        small.append(copy)
    loads = []
    for k in range(SLABS):
        copy = pltpu.make_async_copy(
            image_hbm.at[0, k], padded.at[k, 0:R_DEV, PAD : PAD + CW], image_sem.at[k]
        )
        copy.start()
        loads.append(copy)

    pl.semaphore_wait(barrier, lower_count + 1)
    for step in range(visits - 1, 0, -1):

        @pl.when(visit >= step)
        def _():
            pl.semaphore_signal(
                ready.at[visit], inc=1, device_id=at(visit - step, 1), device_id_type=MESH
            )

        @pl.when((visit >= step) & (row == 0))
        def _():
            pl.semaphore_signal(
                ready.at[visit], inc=1, device_id=at(visit - step, 0), device_id_type=MESH
            )

    edge = pl.multiple_of((1 - row) * (R_DEV - HALO), HALO)
    halo_copies = []
    for k in range(SLABS):
        copy = pltpu.make_async_remote_copy(
            src_ref=image_hbm.at[0, k, pl.ds(edge, HALO), :],
            dst_ref=padded.at[k, R_DEV:ROWS, PAD : PAD + CW],
            send_sem=halo_send.at[k],
            recv_sem=halo_recv.at[k],
            device_id=at(visit, 1 - row),
            device_id_type=MESH,
        )
        copy.start()
        halo_copies.append(copy)

    star_copy.wait()
    stars = star_ref[0]
    own_gram = pack(
        lax.dot_general(
            stars,
            stars,
            (((1,), (1,)), ((), ())),
            precision=HIGHEST,
            preferred_element_type=jnp.float32,
        )
    )
    grams[me] = own_gram

    def gram_down(step, side, target, other_row):
        return pltpu.make_async_remote_copy(
            src_ref=grams.at[me],
            dst_ref=grams.at[me],
            send_sem=gram_send.at[step * rows_count + side],
            recv_sem=gram_recv.at[me],
            device_id=at(target, other_row),
            device_id_type=MESH,
        )

    def gram_up(target, other_row):
        return pltpu.make_async_remote_copy(
            src_ref=pair_sum,
            dst_ref=grams.at[me],
            send_sem=up_send.at[target * rows_count + other_row],
            recv_sem=gram_recv.at[me],
            device_id=at(target, other_row),
            device_id_type=MESH,
        )

    def gram_arrival(other_visit, other_row):
        other = other_visit * rows_count + other_row
        return pltpu.make_async_remote_copy(
            src_ref=grams.at[other],
            dst_ref=grams.at[other],
            send_sem=gram_send.at[0],
            recv_sem=gram_recv.at[other],
            device_id=at(other_visit, other_row),
            device_id_type=MESH,
        )

    pair_copy = gram_down(0, 0, visit, 1 - row)
    pair_copy.start()
    for step in range(visits - 1, 0, -1):

        @pl.when(visit >= step)
        def _():
            gram_down(step, 0, visit - step, row).start()
            gram_down(step, 1, visit - step, 1 - row).start()

    @pl.loop(0, visit)
    def _(other):
        grams[other * rows_count] = jnp.zeros((8, TW), jnp.float32)

    for k in range(SLABS):
        padded[k, :, 0:PAD] = jnp.zeros((ROWS, PAD), jnp.bfloat16)
        padded[k, :, PAD + CW :] = jnp.zeros((ROWS, PAD), jnp.bfloat16)
    for step in range(visits):
        for k in range(SLABS):
            filled = OWN_K + k * HALO_K + NBASIS * HALO
            z[step, filled : OWN_K + (k + 1) * HALO_K, :] = jnp.zeros(
                (HALO_K - NBASIS * HALO, TILES_DEV * TW), jnp.bfloat16
            )
    for copy in small:
        copy.wait()
    tap = iota((NTAPS, 2 * TW), 0)
    lanes = iota((NTAPS, 2 * TW), 1)

    def spread(taps, here, index, there, other):
        one = jnp.where(lanes == jnp.bitwise_and(index, 2 * TW - 1), here, 0.0)
        two = jnp.where(lanes == jnp.bitwise_and(other, 2 * TW - 1), there, 0.0)
        return jnp.dot(taps, (one + two).astype(jnp.bfloat16), preferred_element_type=jnp.float32)

    reversed_taps = spread(column_tap_ref[...], 0.375, -tap, 0.625, -1 - tap)
    for b in range(NBASIS):
        base = jnp.broadcast_to(reversed_taps[b : b + 1, :], (2 * TW, 2 * TW))
        rolled = pltpu.roll(base, 0, 1, stride=1, stride_axis=0)
        band[:, b * TW : (b + 1) * TW] = rolled[:, 0:TW].astype(jnp.bfloat16)

    table = weight_ref[...].astype(jnp.float32)
    cell_visit, cell_ccd = iota(table.shape, 0), iota(table.shape, 1)

    def weight_of(source, k):
        hit = (cell_visit == source) & (cell_ccd == patch * C_DEV + k)
        return jnp.sum(jnp.where(hit, table, 0.0), keepdims=True)

    both = spread(row_tap_ref[...], 0.75, tap - HALF, 0.25, tap + 1 - HALF)
    alone = spread(row_tap_ref[...], 0.75, tap - HALF, 0.0, tap + 1 - HALF)
    lane = iota((R_DEV, TW), 1)
    wide_sub = iota((R_DEV, 2 * TW), 0)
    last = (wide_sub == R_DEV - 1) & (row == rows_count - 1)
    halo_parts = [jnp.zeros((R_DEV, TW), jnp.float32) for _ in range(HALO_K // TW)]
    for b in range(NBASIS):
        base = jnp.where(
            last,
            jnp.broadcast_to(alone[b : b + 1], (R_DEV, 2 * TW)),
            jnp.broadcast_to(both[b : b + 1], (R_DEV, 2 * TW)),
        )
        rolled = pltpu.roll(base, 0, 1, stride=1, stride_axis=0)
        plain[:, b * TW : (b + 1) * TW] = rolled[:, 0:TW]
        low = b % 8 * HALO
        piece = pltpu.roll(rolled[:, TW:], jnp.bitwise_and(low + row * HALO, TW - 1), 1)
        inside = (lane >= low) & (lane < low + HALO)
        halo_parts[b // 8] = jnp.where(inside, piece, halo_parts[b // 8])
    for t, part in enumerate(halo_parts):
        plain[:, (NBASIS + t) * TW : (NBASIS + t + 1) * TW] = part
    sets = iota(coeff_ref.shape, 1)
    for k in range(SLABS):
        picked = jnp.sum(
            jnp.where(sets == choice_ref[0, k], coeff_ref[...], 0.0), axis=1, keepdims=True
        )
        chosen[k] = jnp.broadcast_to(picked * weight_of(visit, k), (NBASIS, TW))

    def add_windows(index, owner):
        entries = []
        for e in range(CAP):
            q = owner * CAP + e
            k = list_ref[0, visit, 0, q]
            start = list_ref[1, visit, 0, q] + (PAD - HALF)
            tile = lax.shift_right_logical(start, 7)
            shift = start - tile * TW
            place = jnp.where(k >= 0, list_ref[2, visit, 0, q] * SLABS + k, -1)
            back = jnp.bitwise_and(TW - shift, TW - 1)
            entries.append((place, jnp.maximum(k, 0), tile, shift, back))
        for first_row, unit in [(r, UNIT) for r in range(0, R_DEV, UNIT)] + [(R_DEV, HALO)]:
            spot = iota((unit, TW), 1)
            left, right = [], []
            for _, k, tile, shift, back in entries:
                parts = []
                for t in range(3):
                    at = (tile + t) * TW
                    piece = padded[k, first_row : first_row + unit, pl.ds(at, TW)]
                    parts.append(pltpu.roll(piece, back, 1))
                keep = spot < TW - shift
                left.append(jnp.where(keep, parts[0], parts[1]))
                right.append(jnp.where(keep, parts[1], parts[2]))
            windows = jnp.concatenate(
                [jnp.concatenate(left, axis=0), jnp.concatenate(right, axis=0)], axis=1
            )
            out = jnp.dot(choose(entries, unit), windows, preferred_element_type=jnp.float32)
            out = out.astype(jnp.bfloat16)
            for p in range(PLACES):
                sums[index, p, first_row : first_row + unit, :] = out[p * unit : (p + 1) * unit]

    def filter_columns(index):
        block = sums[index].reshape(PLACES * ROWS, 2 * TW)
        out = jnp.dot(block, band[...], preferred_element_type=jnp.float32).astype(jnp.bfloat16)
        for p in range(PLACES):
            slot, k = p // SLABS, p % SLABS
            at = slice(slot * TW, (slot + 1) * TW)
            for b in range(NBASIS):
                m = k * NBASIS + b
                part = out[p * ROWS : (p + 1) * ROWS, b * TW : (b + 1) * TW]
                z[index, m * R_DEV : (m + 1) * R_DEV, at] = part[:R_DEV]
                halo_at = OWN_K + k * HALO_K + b * HALO
                z[index, halo_at : halo_at + HALO, at] = part[R_DEV:]

    for copy in loads:
        copy.wait()
    for copy in halo_copies:
        copy.wait_recv()

    def owner_of(step):
        if step == visits - 1:
            return visit
        return step + lax.div(step + visits - visit, visits)

    gram_arrival(visit, 1 - row).wait_recv()
    pair_sum[...] = own_gram + grams[visit * rows_count + 1 - row]
    def prepare(step):
        add_windows(step, owner_of(step))
        filter_columns(step)

    for step in range(visits - 1):
        target = visit + step + 1

        @pl.when(target < visits)
        def _():
            pl.semaphore_wait(ready.at[target], 1 + row)

        @pl.when((target < visits) & (row == 1))
        def _():
            gram_up(target, 0).start()
            gram_up(target, 1).start()

        if step < BEFORE:
            prepare(step)

    for step in range(1, visits):

        @pl.when(visit >= step)
        def _():
            gram_arrival(visit - step, 1).wait_recv()

        @pl.when(visit + step < visits)
        def _():
            for r in range(rows_count):
                gram_arrival(visit + step, r).wait_recv()

    packed = grams[0]
    for s in range(1, members):
        packed = packed + grams[s]
    scales = basis_scales(packed)
    spot = iota((1, TW), 1)
    for k in range(SLABS):
        factors = [scales[b][0:1] * chosen[k, b : b + 1] for b in range(NBASIS)]
        for b in range(NBASIS):
            source, target = slice(b * TW, (b + 1) * TW), (k * NBASIS + b) * TW
            wide = jnp.broadcast_to(factors[b], (R_DEV, TW))
            mixed[:, target : target + TW] = (plain[:, source] * wide).astype(jnp.bfloat16)
        for t in range(HALO_K // TW):
            along = jnp.zeros((1, TW), jnp.float32)
            for b in range(t * 8, min(t * 8 + 8, NBASIS)):
                along = jnp.where(spot >= b % 8 * HALO, factors[b], along)
            source, target = slice((NBASIS + t) * TW, (NBASIS + t + 1) * TW), OWN_K + k * HALO_K + t * TW
            wide = jnp.broadcast_to(along, (R_DEV, TW))
            mixed[:, target : target + TW] = (plain[:, source] * wide).astype(jnp.bfloat16)

    def mix_rows(index, owner):
        out = jnp.dot(mixed[...], z[index], preferred_element_type=jnp.float32)
        out = out.astype(jnp.bfloat16)
        for g in range(TILES_DEV):
            outgoing[owner, g] = out[:, g * TW : (g + 1) * TW]

    tile_copies = []
    for step in range(visits - 1):
        if step >= BEFORE:
            prepare(step)
        owner = owner_of(step)
        mix_rows(step, owner)
        copy = pltpu.make_async_remote_copy(
            src_ref=outgoing.at[owner],
            dst_ref=incoming.at[visit],
            send_sem=tile_send.at[step],
            recv_sem=tile_recv.at[visit],
            device_id={"visit": owner},
            device_id_type=MESH,
        )
        copy.start()
        tile_copies.append(copy)
    prepare(visits - 1)
    mix_rows(visits - 1, visit)

    lower, solved = factor_steps(unpack(packed), stars)
    root = math.sqrt(star_total)
    factor_ref[0] = lower / root
    white_ref[0] = solved * root

    slot_lane = iota((1, list_vec.shape[3]), 1)
    mine = (slot_lane >= visit * CAP) & (slot_lane < visit * CAP + CAP)
    totals = [jnp.zeros((1, 1), jnp.float32) for _ in range(TILES_DEV)]
    for s in range(visits):
        block, slot = list_vec[0, s], list_vec[2, s]
        for g in range(TILES_DEV):
            for k in range(SLABS):
                ones = jnp.where(mine & (block == k) & (slot == g), 1.0, 0.0)
                count = jnp.sum(ones, axis=1, keepdims=True)
                totals[g] = totals[g] + count * weight_of(s, k)
    numerators = [outgoing[visit, g].astype(jnp.float32) for g in range(TILES_DEV)]
    for step in range(1, visits):
        source = lax.rem(visit + step, visits)
        pltpu.make_async_remote_copy(
            src_ref=outgoing.at[source],
            dst_ref=incoming.at[source],
            send_sem=tile_send.at[step - 1],
            recv_sem=tile_recv.at[source],
            device_id={"visit": source},
            device_id_type=MESH,
        ).wait_recv()
        for g in range(TILES_DEV):
            numerators[g] = numerators[g] + incoming[source, g].astype(jnp.float32)
    for g in range(TILES_DEV):
        coadd_ref[0, g] = numerators[g] / totals[g]
    for copy in halo_copies + [pair_copy] + tile_copies:
        copy.wait_send()
    for step in range(1, visits):

        @pl.when(visit >= step)
        def _():
            gram_down(step, 0, visit - step, row).wait_send()
            gram_down(step, 1, visit - step, 1 - row).wait_send()

        @pl.when((visit + step < visits) & (row == 1))
        def _():
            gram_up(visit + step, 0).wait_send()
            gram_up(visit + step, 1).wait_send()


def result_kernel(*refs):
    sources, targets, sem = refs[:3], refs[3:6], refs[6]
    copies = []
    for i, (source, target) in enumerate(zip(sources, targets)):
        copy = pltpu.make_async_copy(source, target, sem.at[i])
        copy.start()
        copies.append(copy)
    for copy in copies:
        copy.wait()


def on_device(
    exposures,
    kernel_choice,
    kernel_coeffs,
    row_taps,
    column_taps,
    visit_weight,
    footprints,
    star_coeffs,
):
    visits = lax.axis_size("visit")
    rows_count = lax.axis_size("row")
    members = visits * rows_count
    star_total = star_coeffs.shape[2] * members
    vmem = pl.BlockSpec(memory_space=pltpu.VMEM)
    anywhere = pl.BlockSpec(memory_space=pl.ANY)
    hbm = pl.BlockSpec(memory_space=pltpu.HBM)
    tiles = pltpu.VMEM((visits, TILES_DEV, R_DEV, TW), jnp.bfloat16)
    dma = pltpu.SemaphoreType.DMA
    operands = (
        kernel_choice,
        footprints,
        visit_weight,
        kernel_coeffs,
        row_taps,
        column_taps,
        star_coeffs,
        exposures,
    )
    results = pl.pallas_call(
        functools.partial(coadd_kernel, visits, rows_count, star_total),
        out_shape=(
            jax.ShapeDtypeStruct((1, TILES_DEV, R_DEV, TW), jnp.float32),
            jax.ShapeDtypeStruct((1, NCOMP, NCOMP), jnp.float32),
            jax.ShapeDtypeStruct(star_coeffs.shape, jnp.float32),
        ),
        in_specs=[hbm] * 8,
        out_specs=(vmem, vmem, vmem),
        scratch_shapes=[
            pltpu.SMEM(kernel_choice.shape, jnp.int32),
            pltpu.SMEM(footprints.shape, jnp.int32),
            pltpu.VMEM(footprints.shape, jnp.int32),
            pltpu.VMEM(visit_weight.shape, jnp.bfloat16),
            pltpu.VMEM(kernel_coeffs.shape, jnp.float32),
            pltpu.VMEM(row_taps.shape, jnp.bfloat16),
            pltpu.VMEM(column_taps.shape, jnp.bfloat16),
            pltpu.VMEM(star_coeffs.shape, jnp.float32),
            pltpu.VMEM((SLABS, ROWS, CW + 2 * PAD), jnp.bfloat16),
            pltpu.VMEM((visits, PLACES, ROWS, 2 * TW), jnp.bfloat16),
            pltpu.VMEM((2 * TW, NBASIS * TW), jnp.bfloat16),
            pltpu.VMEM((visits, ALL_K, TILES_DEV * TW), jnp.bfloat16),
            pltpu.VMEM((R_DEV, NBASIS * TW + HALO_K), jnp.float32),
            pltpu.VMEM((SLABS, NBASIS, TW), jnp.float32),
            pltpu.VMEM((R_DEV, ALL_K), jnp.bfloat16),
            pltpu.VMEM((members, 8, TW), jnp.float32),
            pltpu.VMEM((8, TW), jnp.float32),
            tiles,
            tiles,
            dma((7,)),
            dma,
            dma((SLABS,)),
            dma((SLABS,)),
            dma((SLABS,)),
            dma((members,)),
            dma((members,)),
            dma((members,)),
            pltpu.SemaphoreType.REGULAR((visits,)),
            dma((visits,)),
            dma((visits,)),
        ],
        compiler_params=pltpu.CompilerParams(
            vmem_limit_bytes=VMEM_LIMIT, collective_id=0, has_side_effects=True
        ),
        name="coadd",
    )(*[pltpu.with_memory_space_constraint(x, pltpu.HBM) for x in operands])
    return pl.pallas_call(
        result_kernel,
        out_shape=tuple(jax.ShapeDtypeStruct(part.shape, part.dtype) for part in results),
        in_specs=[anywhere] * 3,
        out_specs=(anywhere,) * 3,
        scratch_shapes=[dma((3,))],
        compiler_params=pltpu.CompilerParams(vmem_limit_bytes=4 * 1024 * 1024),
        name="results",
    )(*results)


def solution(mesh):
    in_specs = (
        P(("blk", "visit"), "patch", "row", None),
        P(("blk", "visit"), "patch"),
        P(),
        P(),
        P(),
        P("blk", None),
        P(None, "blk", "patch", None),
        P(("blk", "patch"), None, ("visit", "row")),
    )
    out_specs = (
        P(("blk", "patch"), "visit", "row", None),
        P(("blk", "patch"), None, None),
        P(("blk", "patch"), None, ("visit", "row")),
    )
    return jax.shard_map(
        on_device, mesh=mesh, in_specs=in_specs, out_specs=out_specs, check_vma=False
    )
```

```python
import functools
import math

import jax
import jax.numpy as jnp
from jax import lax
from jax.experimental import pallas as pl
from jax.experimental.pallas import tpu as pltpu
from jax.sharding import PartitionSpec as P

NBASIS = 9
NTAPS = 21
C_DEV = 2
R_DEV = 128
CW = 4096
TW = 128
CAP = 8
TILES_DEV = 2
HALF = 10
SLABS = 2
HALO = 16
ROWS = R_DEV + HALO
NCOMP = 32
PAD = 128
PLACES = TILES_DEV * SLABS
PAIRS = SLABS * NBASIS
OWN_K = PAIRS * R_DEV
HALO_K = 2 * TW
ALL_K = OWN_K + SLABS * HALO_K
BEFORE = 2
UNIT = 32
HIGHEST = lax.Precision.HIGHEST
VMEM_LIMIT = 48 * 1024 * 1024
MESH = pl.DeviceIdType.MESH


def iota(shape, axis):
    return lax.broadcasted_iota(jnp.int32, shape, axis)


def factor_steps(gram):
    side = jnp.where(iota((NCOMP, NCOMP), 0) == iota((NCOMP, NCOMP), 1), 1.0, 0.0)
    both = jnp.concatenate([gram, side, side, side], axis=1)
    groups = NCOMP // 8
    full = (8, TW)
    sub, lane = iota(full, 0), iota(full, 1)
    rows = [both[8 * g : 8 * g + 8] for g in range(groups)]
    lower = [jnp.zeros(full, jnp.float32) for _ in range(groups)]
    for p in range(groups):
        columns = [
            {g: jnp.broadcast_to(rows[g][:, 8 * p + j : 8 * p + j + 1], full) for g in range(p, groups)}
            for j in range(8)
        ]
        for j in range(8):
            inverse = lax.rsqrt(jnp.broadcast_to(columns[j][p][j : j + 1], full))
            scaled = {g: columns[j][g] * inverse for g in range(p, groups)}
            for k in range(j + 1, 8):
                ratio = jnp.broadcast_to(scaled[p][k : k + 1], full)
                for g in range(p, groups):
                    columns[k][g] = columns[k][g] - scaled[g] * ratio
            scaled[p] = jnp.where(sub >= j, scaled[p], 0.0)
            for g in range(p, groups):
                lower[g] = jnp.where(lane == 8 * p + j, scaled[g], lower[g])
            solved = jnp.broadcast_to(rows[p][j : j + 1], full) * inverse
            rows[p] = jnp.where(
                sub == j, solved, rows[p] - jnp.where(sub > j, scaled[p], 0.0) * solved
            )
            for g in range(p + 1, groups):
                rows[g] = rows[g] - scaled[g] * solved
    inverse = jnp.concatenate([r[:, NCOMP : 2 * NCOMP] for r in rows], axis=0)
    return jnp.concatenate([part[:, :NCOMP] for part in lower], axis=0), inverse


def pack(square):
    return jnp.concatenate([square[a : a + 8] for a in range(0, NCOMP, 8)], axis=1)


def unpack(packed):
    return jnp.concatenate([packed[:, a : a + NCOMP] for a in range(0, TW, NCOMP)], axis=0)


def basis_scales(packed):
    full = (8, TW)
    columns = [jnp.broadcast_to(packed[:, j : j + 1], full) for j in range(8)]
    ninth = [jnp.broadcast_to(packed[0:1, NCOMP + j : NCOMP + j + 1], full) for j in range(NBASIS)]
    pivots = []
    for j in range(8):
        pivot = jnp.broadcast_to(columns[j][j : j + 1], full)
        pivots.append(pivot)
        inverse = 1.0 / pivot
        for k in range(j + 1, 8):
            ratio = jnp.broadcast_to(columns[j][k : k + 1], full) * inverse
            columns[k] = columns[k] - columns[j] * ratio
            ninth[k] = ninth[k] - ninth[j] * ratio
        ninth[8] = ninth[8] - ninth[j] * (ninth[j] * inverse)
    pivots.append(ninth[8])
    total = pivots[0]
    for pivot in pivots[1:]:
        total = total + pivot
    norm = 1.0 / jnp.sqrt(total / NBASIS)
    return [jnp.sqrt(pivot) * norm for pivot in pivots]


def choose(entries, unit):
    shape = (PLACES * unit, CAP * unit)
    sub, lane = iota(shape, 0), iota(shape, 1)
    spot = iota((1, CAP * unit), 1)
    place = jnp.full(spot.shape, -1, jnp.int32)
    for e, entry in enumerate(entries):
        place = jnp.where(spot >= e * unit, entry[0], place)
    bits = unit.bit_length() - 1
    same = jnp.bitwise_and(sub, unit - 1) == jnp.bitwise_and(lane, unit - 1)
    hit = same & (lax.shift_right_logical(sub, bits) == place)
    return jnp.where(hit, 1.0, 0.0).astype(jnp.bfloat16)


def coadd_kernel(
    visits,
    rows_count,
    star_total,
    choice_hbm,
    list_hbm,
    weight_hbm,
    coeff_hbm,
    row_tap_hbm,
    column_tap_hbm,
    star_hbm,
    image_hbm,
    coadd_ref,
    factor_ref,
    white_ref,
    choice_ref,
    list_ref,
    list_vec,
    weight_ref,
    coeff_ref,
    row_tap_ref,
    column_tap_ref,
    star_ref,
    padded,
    sums,
    band,
    z,
    plain,
    chosen,
    mixed,
    grams,
    pair_sum,
    outgoing,
    incoming,
    small_sem,
    star_sem,
    image_sem,
    halo_send,
    halo_recv,
    gram_send,
    gram_recv,
    up_send,
    ready,
    tile_send,
    tile_recv,
):
    visit = lax.axis_index("visit")
    row = lax.axis_index("row")
    patch = lax.axis_index("patch")
    members = visits * rows_count
    me = visit * rows_count + row
    lower_count = visit * rows_count

    def at(other_visit, other_row):
        return {"visit": other_visit, "row": other_row}

    barrier = pltpu.get_barrier_semaphore()
    pl.semaphore_signal(barrier, inc=1, device_id=at(visit, 1 - row), device_id_type=MESH)
    for step in range(visits - 1, 0, -1):

        @pl.when(visit + step < visits)
        def _():
            for r in range(rows_count):
                pl.semaphore_signal(barrier, inc=1, device_id=at(visit + step, r), device_id_type=MESH)

    star_copy = pltpu.make_async_copy(star_hbm, star_ref, star_sem)
    star_copy.start()
    loads = []
    for k in range(SLABS):
        copy = pltpu.make_async_copy(
            image_hbm.at[0, k], padded.at[k, 0:R_DEV, PAD : PAD + CW], image_sem.at[k]
        )
        copy.start()
        loads.append(copy)

    pl.semaphore_wait(barrier, lower_count + 1)
    for step in range(visits - 1, 0, -1):

        @pl.when(visit >= step)
        def _():
            pl.semaphore_signal(
                ready.at[visit], inc=1, device_id=at(visit - step, 1), device_id_type=MESH
            )

        @pl.when((visit >= step) & (row == 0))
        def _():
            pl.semaphore_signal(
                ready.at[visit], inc=1, device_id=at(visit - step, 0), device_id_type=MESH
            )

    small = []
    for source, target in (
        (column_tap_hbm, column_tap_ref),
        (row_tap_hbm, row_tap_ref),
        (coeff_hbm, coeff_ref),
        (weight_hbm, weight_ref),
        (list_hbm, list_vec),
        (choice_hbm, choice_ref),
        (list_hbm, list_ref),
    ):
        copy = pltpu.make_async_copy(source, target, small_sem.at[len(small)])
        copy.start()
        small.append(copy)
    edge = pl.multiple_of((1 - row) * (R_DEV - HALO), HALO)
    halo_copies = []
    for k in range(SLABS):
        copy = pltpu.make_async_remote_copy(
            src_ref=image_hbm.at[0, k, pl.ds(edge, HALO), :],
            dst_ref=padded.at[k, R_DEV:ROWS, PAD : PAD + CW],
            send_sem=halo_send.at[k],
            recv_sem=halo_recv.at[k],
            device_id=at(visit, 1 - row),
            device_id_type=MESH,
        )
        copy.start()
        halo_copies.append(copy)

    star_copy.wait()
    stars = star_ref[0]
    own_gram = pack(
        lax.dot_general(
            stars,
            stars,
            (((1,), (1,)), ((), ())),
            precision=HIGHEST,
            preferred_element_type=jnp.float32,
        )
    )
    grams[me] = own_gram

    def gram_down(step, side, target, other_row):
        return pltpu.make_async_remote_copy(
            src_ref=grams.at[me],
            dst_ref=grams.at[me],
            send_sem=gram_send.at[step * rows_count + side],
            recv_sem=gram_recv.at[me],
            device_id=at(target, other_row),
            device_id_type=MESH,
        )

    def gram_up(target, other_row):
        return pltpu.make_async_remote_copy(
            src_ref=pair_sum,
            dst_ref=grams.at[me],
            send_sem=up_send.at[target * rows_count + other_row],
            recv_sem=gram_recv.at[me],
            device_id=at(target, other_row),
            device_id_type=MESH,
        )

    def gram_arrival(other_visit, other_row):
        other = other_visit * rows_count + other_row
        return pltpu.make_async_remote_copy(
            src_ref=grams.at[other],
            dst_ref=grams.at[other],
            send_sem=gram_send.at[0],
            recv_sem=gram_recv.at[other],
            device_id=at(other_visit, other_row),
            device_id_type=MESH,
        )

    pair_copy = gram_down(0, 0, visit, 1 - row)
    pair_copy.start()
    for step in range(visits - 1, 0, -1):

        @pl.when(visit >= step)
        def _():
            gram_down(step, 0, visit - step, row).start()
            gram_down(step, 1, visit - step, 1 - row).start()

    @pl.loop(0, visit)
    def _(other):
        grams[other * rows_count] = jnp.zeros((8, TW), jnp.float32)

    for k in range(SLABS):
        padded[k, :, 0:PAD] = jnp.zeros((ROWS, PAD), jnp.bfloat16)
        padded[k, :, PAD + CW :] = jnp.zeros((ROWS, PAD), jnp.bfloat16)
    for step in range(visits):
        for k in range(SLABS):
            filled = OWN_K + k * HALO_K + NBASIS * HALO
            z[step, filled : OWN_K + (k + 1) * HALO_K, :] = jnp.zeros(
                (HALO_K - NBASIS * HALO, TILES_DEV * TW), jnp.bfloat16
            )
    for copy in small:
        copy.wait()
    tap = iota((NTAPS, 2 * TW), 0)
    lanes = iota((NTAPS, 2 * TW), 1)

    def spread(taps, here, index, there, other):
        one = jnp.where(lanes == jnp.bitwise_and(index, 2 * TW - 1), here, 0.0)
        two = jnp.where(lanes == jnp.bitwise_and(other, 2 * TW - 1), there, 0.0)
        return jnp.dot(taps, (one + two).astype(jnp.bfloat16), preferred_element_type=jnp.float32)

    reversed_taps = spread(column_tap_ref[...], 0.375, -tap, 0.625, -1 - tap)
    for b in range(NBASIS):
        base = jnp.broadcast_to(reversed_taps[b : b + 1, :], (2 * TW, 2 * TW))
        rolled = pltpu.roll(base, 0, 1, stride=1, stride_axis=0)
        band[:, b * TW : (b + 1) * TW] = rolled[:, 0:TW].astype(jnp.bfloat16)

    table = weight_ref[...].astype(jnp.float32)
    cell_visit, cell_ccd = iota(table.shape, 0), iota(table.shape, 1)

    def weight_of(source, k):
        hit = (cell_visit == source) & (cell_ccd == patch * C_DEV + k)
        return jnp.sum(jnp.where(hit, table, 0.0), keepdims=True)

    both = spread(row_tap_ref[...], 0.75, tap - HALF, 0.25, tap + 1 - HALF)
    alone = spread(row_tap_ref[...], 0.75, tap - HALF, 0.0, tap + 1 - HALF)
    lane = iota((R_DEV, TW), 1)
    wide_sub = iota((R_DEV, 2 * TW), 0)
    last = (wide_sub == R_DEV - 1) & (row == rows_count - 1)
    halo_parts = [jnp.zeros((R_DEV, TW), jnp.float32) for _ in range(HALO_K // TW)]
    for b in range(NBASIS):
        base = jnp.where(
            last,
            jnp.broadcast_to(alone[b : b + 1], (R_DEV, 2 * TW)),
            jnp.broadcast_to(both[b : b + 1], (R_DEV, 2 * TW)),
        )
        rolled = pltpu.roll(base, 0, 1, stride=1, stride_axis=0)
        plain[:, b * TW : (b + 1) * TW] = rolled[:, 0:TW]
        low = b % 8 * HALO
        piece = pltpu.roll(rolled[:, TW:], jnp.bitwise_and(low + row * HALO, TW - 1), 1)
        inside = (lane >= low) & (lane < low + HALO)
        halo_parts[b // 8] = jnp.where(inside, piece, halo_parts[b // 8])
    for t, part in enumerate(halo_parts):
        plain[:, (NBASIS + t) * TW : (NBASIS + t + 1) * TW] = part
    sets = iota(coeff_ref.shape, 1)
    for k in range(SLABS):
        picked = jnp.sum(
            jnp.where(sets == choice_ref[0, k], coeff_ref[...], 0.0), axis=1, keepdims=True
        )
        chosen[k] = jnp.broadcast_to(picked * weight_of(visit, k), (NBASIS, TW))

    def add_windows(index, owner):
        entries = []
        for e in range(CAP):
            q = owner * CAP + e
            k = list_ref[0, visit, 0, q]
            start = list_ref[1, visit, 0, q] + (PAD - HALF)
            tile = lax.shift_right_logical(start, 7)
            shift = start - tile * TW
            place = jnp.where(k >= 0, list_ref[2, visit, 0, q] * SLABS + k, -1)
            back = jnp.bitwise_and(TW - shift, TW - 1)
            entries.append((place, jnp.maximum(k, 0), tile, shift, back))
        for first_row, unit in [(r, UNIT) for r in range(0, R_DEV, UNIT)] + [(R_DEV, HALO)]:
            spot = iota((unit, TW), 1)
            left, right = [], []
            for _, k, tile, shift, back in entries:
                parts = []
                for t in range(3):
                    at = (tile + t) * TW
                    piece = padded[k, first_row : first_row + unit, pl.ds(at, TW)]
                    parts.append(pltpu.roll(piece, back, 1))
                keep = spot < TW - shift
                left.append(jnp.where(keep, parts[0], parts[1]))
                right.append(jnp.where(keep, parts[1], parts[2]))
            windows = jnp.concatenate(
                [jnp.concatenate(left, axis=0), jnp.concatenate(right, axis=0)], axis=1
            )
            out = jnp.dot(choose(entries, unit), windows, preferred_element_type=jnp.float32)
            out = out.astype(jnp.bfloat16)
            for p in range(PLACES):
                sums[index, p, first_row : first_row + unit, :] = out[p * unit : (p + 1) * unit]

    def filter_columns(index):
        block = sums[index].reshape(PLACES * ROWS, 2 * TW)
        out = jnp.dot(block, band[...], preferred_element_type=jnp.float32).astype(jnp.bfloat16)
        for p in range(PLACES):
            slot, k = p // SLABS, p % SLABS
            at = slice(slot * TW, (slot + 1) * TW)
            for b in range(NBASIS):
                m = k * NBASIS + b
                part = out[p * ROWS : (p + 1) * ROWS, b * TW : (b + 1) * TW]
                z[index, m * R_DEV : (m + 1) * R_DEV, at] = part[:R_DEV]
                halo_at = OWN_K + k * HALO_K + b * HALO
                z[index, halo_at : halo_at + HALO, at] = part[R_DEV:]

    for copy in loads:
        copy.wait()
    for copy in halo_copies:
        copy.wait_recv()

    def owner_of(step):
        if step == visits - 1:
            return visit
        later = lax.div(visit + visits - 1, visits)
        if step == 0:
            return 1 - later
        place = step - later
        above = visits - 1 - visit
        up = lax.div(above - place + visits - 1, visits)
        return up * (visit + 1 + place) + (1 - up) * (visit - 1 - place + above)

    gram_arrival(visit, 1 - row).wait_recv()
    pair_sum[...] = own_gram + grams[visit * rows_count + 1 - row]

    def prepare(step):
        add_windows(step, owner_of(step))
        filter_columns(step)

    for step in range(visits - 1):
        target = visit + step + 1

        @pl.when(target < visits)
        def _():
            pl.semaphore_wait(ready.at[target], 1 + row)

        @pl.when((target < visits) & (row == 1))
        def _():
            gram_up(target, 0).start()
            gram_up(target, 1).start()

        if step < BEFORE:
            prepare(step)

    for step in range(1, visits):

        @pl.when(visit >= step)
        def _():
            gram_arrival(visit - step, 1).wait_recv()

        @pl.when(visit + step < visits)
        def _():
            for r in range(rows_count):
                gram_arrival(visit + step, r).wait_recv()

    packed = grams[0]
    for s in range(1, members):
        packed = packed + grams[s]
    scales = basis_scales(packed)
    spot = iota((1, TW), 1)
    for k in range(SLABS):
        factors = [scales[b][0:1] * chosen[k, b : b + 1] for b in range(NBASIS)]
        for b in range(NBASIS):
            source, target = slice(b * TW, (b + 1) * TW), (k * NBASIS + b) * TW
            wide = jnp.broadcast_to(factors[b], (R_DEV, TW))
            mixed[:, target : target + TW] = (plain[:, source] * wide).astype(jnp.bfloat16)
        for t in range(HALO_K // TW):
            along = jnp.zeros((1, TW), jnp.float32)
            for b in range(t * 8, min(t * 8 + 8, NBASIS)):
                along = jnp.where(spot >= b % 8 * HALO, factors[b], along)
            source, target = slice((NBASIS + t) * TW, (NBASIS + t + 1) * TW), OWN_K + k * HALO_K + t * TW
            wide = jnp.broadcast_to(along, (R_DEV, TW))
            mixed[:, target : target + TW] = (plain[:, source] * wide).astype(jnp.bfloat16)

    def mix_rows(index, owner):
        out = jnp.dot(mixed[...], z[index], preferred_element_type=jnp.float32)
        out = out.astype(jnp.bfloat16)
        for g in range(TILES_DEV):
            outgoing[owner, g] = out[:, g * TW : (g + 1) * TW]

    tile_copies = []
    for step in range(visits - 1):
        if step >= BEFORE:
            prepare(step)
        owner = owner_of(step)
        mix_rows(step, owner)
        copy = pltpu.make_async_remote_copy(
            src_ref=outgoing.at[owner],
            dst_ref=incoming.at[visit],
            send_sem=tile_send.at[step],
            recv_sem=tile_recv.at[visit],
            device_id={"visit": owner},
            device_id_type=MESH,
        )
        copy.start()
        tile_copies.append(copy)
    prepare(visits - 1)
    mix_rows(visits - 1, visit)

    lower, inverse = factor_steps(unpack(packed))
    solved = jnp.dot(inverse, stars, precision=HIGHEST, preferred_element_type=jnp.float32)
    root = math.sqrt(star_total)
    factor_ref[0] = lower / root
    white_ref[0] = solved * root

    slot_lane = iota((1, list_vec.shape[3]), 1)
    mine = (slot_lane >= visit * CAP) & (slot_lane < visit * CAP + CAP)
    totals = [jnp.zeros((1, 1), jnp.float32) for _ in range(TILES_DEV)]
    for s in range(visits):
        block, slot = list_vec[0, s], list_vec[2, s]
        for g in range(TILES_DEV):
            for k in range(SLABS):
                ones = jnp.where(mine & (block == k) & (slot == g), 1.0, 0.0)
                count = jnp.sum(ones, axis=1, keepdims=True)
                totals[g] = totals[g] + count * weight_of(s, k)
    numerators = [outgoing[visit, g].astype(jnp.float32) for g in range(TILES_DEV)]
    for step in range(1, visits):
        source = lax.rem(visit + step, visits)
        pltpu.make_async_remote_copy(
            src_ref=outgoing.at[source],
            dst_ref=incoming.at[source],
            send_sem=tile_send.at[step - 1],
            recv_sem=tile_recv.at[source],
            device_id={"visit": source},
            device_id_type=MESH,
        ).wait_recv()
        for g in range(TILES_DEV):
            numerators[g] = numerators[g] + incoming[source, g].astype(jnp.float32)
    for g in range(TILES_DEV):
        coadd_ref[0, g] = numerators[g] / totals[g]
    for copy in halo_copies + [pair_copy] + tile_copies:
        copy.wait_send()
    for step in range(1, visits):

        @pl.when(visit >= step)
        def _():
            gram_down(step, 0, visit - step, row).wait_send()
            gram_down(step, 1, visit - step, 1 - row).wait_send()

        @pl.when((visit + step < visits) & (row == 1))
        def _():
            gram_up(visit + step, 0).wait_send()
            gram_up(visit + step, 1).wait_send()


def result_kernel(*refs):
    sources, targets, sem = refs[:3], refs[3:6], refs[6]
    copies = []
    for i, (source, target) in enumerate(zip(sources, targets)):
        copy = pltpu.make_async_copy(source, target, sem.at[i])
        copy.start()
        copies.append(copy)
    for copy in copies:
        copy.wait()


def on_device(
    exposures,
    kernel_choice,
    kernel_coeffs,
    row_taps,
    column_taps,
    visit_weight,
    footprints,
    star_coeffs,
):
    visits = lax.axis_size("visit")
    rows_count = lax.axis_size("row")
    members = visits * rows_count
    star_total = star_coeffs.shape[2] * members
    vmem = pl.BlockSpec(memory_space=pltpu.VMEM)
    anywhere = pl.BlockSpec(memory_space=pl.ANY)
    hbm = pl.BlockSpec(memory_space=pltpu.HBM)
    tiles = pltpu.VMEM((visits, TILES_DEV, R_DEV, TW), jnp.bfloat16)
    dma = pltpu.SemaphoreType.DMA
    operands = (
        kernel_choice,
        footprints,
        visit_weight,
        kernel_coeffs,
        row_taps,
        column_taps,
        star_coeffs,
        exposures,
    )
    results = pl.pallas_call(
        functools.partial(coadd_kernel, visits, rows_count, star_total),
        out_shape=(
            jax.ShapeDtypeStruct((1, TILES_DEV, R_DEV, TW), jnp.float32),
            jax.ShapeDtypeStruct((1, NCOMP, NCOMP), jnp.float32),
            jax.ShapeDtypeStruct(star_coeffs.shape, jnp.float32),
        ),
        in_specs=[hbm] * 8,
        out_specs=(vmem, vmem, vmem),
        scratch_shapes=[
            pltpu.SMEM(kernel_choice.shape, jnp.int32),
            pltpu.SMEM(footprints.shape, jnp.int32),
            pltpu.VMEM(footprints.shape, jnp.int32),
            pltpu.VMEM(visit_weight.shape, jnp.bfloat16),
            pltpu.VMEM(kernel_coeffs.shape, jnp.float32),
            pltpu.VMEM(row_taps.shape, jnp.bfloat16),
            pltpu.VMEM(column_taps.shape, jnp.bfloat16),
            pltpu.VMEM(star_coeffs.shape, jnp.float32),
            pltpu.VMEM((SLABS, ROWS, CW + 2 * PAD), jnp.bfloat16),
            pltpu.VMEM((visits, PLACES, ROWS, 2 * TW), jnp.bfloat16),
            pltpu.VMEM((2 * TW, NBASIS * TW), jnp.bfloat16),
            pltpu.VMEM((visits, ALL_K, TILES_DEV * TW), jnp.bfloat16),
            pltpu.VMEM((R_DEV, NBASIS * TW + HALO_K), jnp.float32),
            pltpu.VMEM((SLABS, NBASIS, TW), jnp.float32),
            pltpu.VMEM((R_DEV, ALL_K), jnp.bfloat16),
            pltpu.VMEM((members, 8, TW), jnp.float32),
            pltpu.VMEM((8, TW), jnp.float32),
            tiles,
            tiles,
            dma((7,)),
            dma,
            dma((SLABS,)),
            dma((SLABS,)),
            dma((SLABS,)),
            dma((members,)),
            dma((members,)),
            dma((members,)),
            pltpu.SemaphoreType.REGULAR((visits,)),
            dma((visits,)),
            dma((visits,)),
        ],
        compiler_params=pltpu.CompilerParams(
            vmem_limit_bytes=VMEM_LIMIT, collective_id=0, has_side_effects=True
        ),
        name="coadd",
    )(*[pltpu.with_memory_space_constraint(x, pltpu.HBM) for x in operands])
    return pl.pallas_call(
        result_kernel,
        out_shape=tuple(jax.ShapeDtypeStruct(part.shape, part.dtype) for part in results),
        in_specs=[anywhere] * 3,
        out_specs=(anywhere,) * 3,
        scratch_shapes=[dma((3,))],
        compiler_params=pltpu.CompilerParams(vmem_limit_bytes=4 * 1024 * 1024),
        name="results",
    )(*results)


def solution(mesh):
    in_specs = (
        P(("blk", "visit"), "patch", "row", None),
        P(("blk", "visit"), "patch"),
        P(),
        P(),
        P(),
        P("blk", None),
        P(None, "blk", "patch", None),
        P(("blk", "patch"), None, ("visit", "row")),
    )
    out_specs = (
        P(("blk", "patch"), "visit", "row", None),
        P(("blk", "patch"), None, None),
        P(("blk", "patch"), None, ("visit", "row")),
    )
    return jax.shard_map(
        on_device, mesh=mesh, in_specs=in_specs, out_specs=out_specs, check_vma=False
    )
```

```python
import functools
import math

import jax
import jax.numpy as jnp
from jax import lax
from jax.experimental import pallas as pl
from jax.experimental.pallas import tpu as pltpu
from jax.sharding import PartitionSpec as P

NBASIS = 9
NTAPS = 21
C_DEV = 2
R_DEV = 128
CW = 4096
TW = 128
CAP = 8
TILES_DEV = 2
HALF = 10
SLABS = 2
HALO = 16
ROWS = R_DEV + HALO
NCOMP = 32
PAD = 128
PLACES = TILES_DEV * SLABS
PAIRS = SLABS * NBASIS
OWN_K = PAIRS * R_DEV
HALO_K = 2 * TW
ALL_K = OWN_K + SLABS * HALO_K
BEFORE = 1
UNIT = 32
HIGHEST = lax.Precision.HIGHEST
VMEM_LIMIT = 48 * 1024 * 1024
MESH = pl.DeviceIdType.MESH


def iota(shape, axis):
    return lax.broadcasted_iota(jnp.int32, shape, axis)


def factor_steps(gram):
    side = jnp.where(iota((NCOMP, NCOMP), 0) == iota((NCOMP, NCOMP), 1), 1.0, 0.0)
    both = jnp.concatenate([gram, side, side, side], axis=1)
    groups = NCOMP // 8
    full = (8, TW)
    sub, lane = iota(full, 0), iota(full, 1)
    rows = [both[8 * g : 8 * g + 8] for g in range(groups)]
    lower = [jnp.zeros(full, jnp.float32) for _ in range(groups)]
    for p in range(groups):
        columns = [
            {g: jnp.broadcast_to(rows[g][:, 8 * p + j : 8 * p + j + 1], full) for g in range(p, groups)}
            for j in range(8)
        ]
        for j in range(8):
            inverse = lax.rsqrt(jnp.broadcast_to(columns[j][p][j : j + 1], full))
            scaled = {g: columns[j][g] * inverse for g in range(p, groups)}
            for k in range(j + 1, 8):
                ratio = jnp.broadcast_to(scaled[p][k : k + 1], full)
                for g in range(p, groups):
                    columns[k][g] = columns[k][g] - scaled[g] * ratio
            scaled[p] = jnp.where(sub >= j, scaled[p], 0.0)
            for g in range(p, groups):
                lower[g] = jnp.where(lane == 8 * p + j, scaled[g], lower[g])
            solved = jnp.broadcast_to(rows[p][j : j + 1], full) * inverse
            rows[p] = jnp.where(
                sub == j, solved, rows[p] - jnp.where(sub > j, scaled[p], 0.0) * solved
            )
            for g in range(p + 1, groups):
                rows[g] = rows[g] - scaled[g] * solved
    inverse = jnp.concatenate([r[:, NCOMP : 2 * NCOMP] for r in rows], axis=0)
    return jnp.concatenate([part[:, :NCOMP] for part in lower], axis=0), inverse


def pack(square):
    return jnp.concatenate([square[a : a + 8] for a in range(0, NCOMP, 8)], axis=1)


def unpack(packed):
    return jnp.concatenate([packed[:, a : a + NCOMP] for a in range(0, TW, NCOMP)], axis=0)


def basis_scales(packed):
    full = (8, TW)
    columns = [jnp.broadcast_to(packed[:, j : j + 1], full) for j in range(8)]
    ninth = [jnp.broadcast_to(packed[0:1, NCOMP + j : NCOMP + j + 1], full) for j in range(NBASIS)]
    pivots = []
    for j in range(8):
        pivot = jnp.broadcast_to(columns[j][j : j + 1], full)
        pivots.append(pivot)
        inverse = 1.0 / pivot
        for k in range(j + 1, 8):
            ratio = jnp.broadcast_to(columns[j][k : k + 1], full) * inverse
            columns[k] = columns[k] - columns[j] * ratio
            ninth[k] = ninth[k] - ninth[j] * ratio
        ninth[8] = ninth[8] - ninth[j] * (ninth[j] * inverse)
    pivots.append(ninth[8])
    total = pivots[0]
    for pivot in pivots[1:]:
        total = total + pivot
    norm = 1.0 / jnp.sqrt(total / NBASIS)
    return [jnp.sqrt(pivot) * norm for pivot in pivots]


def choose(entries, unit):
    shape = (PLACES * unit, CAP * unit)
    sub, lane = iota(shape, 0), iota(shape, 1)
    spot = iota((1, CAP * unit), 1)
    place = jnp.full(spot.shape, -1, jnp.int32)
    for e, entry in enumerate(entries):
        place = jnp.where(spot >= e * unit, entry[0], place)
    bits = unit.bit_length() - 1
    same = jnp.bitwise_and(sub, unit - 1) == jnp.bitwise_and(lane, unit - 1)
    hit = same & (lax.shift_right_logical(sub, bits) == place)
    return jnp.where(hit, 1.0, 0.0).astype(jnp.bfloat16)


def coadd_kernel(
    visits,
    rows_count,
    star_total,
    choice_hbm,
    list_hbm,
    weight_hbm,
    coeff_hbm,
    row_tap_hbm,
    column_tap_hbm,
    star_hbm,
    image_hbm,
    coadd_ref,
    factor_ref,
    white_ref,
    choice_ref,
    list_ref,
    list_vec,
    weight_ref,
    coeff_ref,
    row_tap_ref,
    column_tap_ref,
    star_ref,
    padded,
    sums,
    band,
    z,
    plain,
    chosen,
    products,
    mixed,
    grams,
    pair_sum,
    outgoing,
    incoming,
    small_sem,
    star_sem,
    image_sem,
    halo_send,
    halo_recv,
    gram_send,
    gram_recv,
    up_send,
    ready,
    tile_send,
    tile_recv,
):
    visit = lax.axis_index("visit")
    row = lax.axis_index("row")
    patch = lax.axis_index("patch")
    members = visits * rows_count
    me = visit * rows_count + row
    lower_count = visit * rows_count

    def at(other_visit, other_row):
        return {"visit": other_visit, "row": other_row}

    barrier = pltpu.get_barrier_semaphore()
    pl.semaphore_signal(barrier, inc=1, device_id=at(visit, 1 - row), device_id_type=MESH)
    for step in range(visits - 1, 0, -1):

        @pl.when(visit + step < visits)
        def _():
            for r in range(rows_count):
                pl.semaphore_signal(barrier, inc=1, device_id=at(visit + step, r), device_id_type=MESH)

    star_copy = pltpu.make_async_copy(star_hbm, star_ref, star_sem)
    star_copy.start()
    loads = []
    for k in range(SLABS):
        copy = pltpu.make_async_copy(
            image_hbm.at[0, k], padded.at[k, 0:R_DEV, PAD : PAD + CW], image_sem.at[k]
        )
        copy.start()
        loads.append(copy)

    pl.semaphore_wait(barrier, lower_count + 1)
    for step in range(visits - 1, 0, -1):

        @pl.when(visit >= step)
        def _():
            pl.semaphore_signal(
                ready.at[visit], inc=1, device_id=at(visit - step, 1), device_id_type=MESH
            )

        @pl.when((visit >= step) & (row == 0))
        def _():
            pl.semaphore_signal(
                ready.at[visit], inc=1, device_id=at(visit - step, 0), device_id_type=MESH
            )

    small = []
    for source, target in (
        (column_tap_hbm, column_tap_ref),
        (row_tap_hbm, row_tap_ref),
        (coeff_hbm, coeff_ref),
        (weight_hbm, weight_ref),
        (list_hbm, list_vec),
        (choice_hbm, choice_ref),
        (list_hbm, list_ref),
    ):
        copy = pltpu.make_async_copy(source, target, small_sem.at[len(small)])
        copy.start()
        small.append(copy)
    edge = pl.multiple_of((1 - row) * (R_DEV - HALO), HALO)
    halo_copies = []
    for k in range(SLABS):
        copy = pltpu.make_async_remote_copy(
            src_ref=image_hbm.at[0, k, pl.ds(edge, HALO), :],
            dst_ref=padded.at[k, R_DEV:ROWS, PAD : PAD + CW],
            send_sem=halo_send.at[k],
            recv_sem=halo_recv.at[k],
            device_id=at(visit, 1 - row),
            device_id_type=MESH,
        )
        copy.start()
        halo_copies.append(copy)

    star_copy.wait()
    stars = star_ref[0]
    own_gram = pack(
        lax.dot_general(
            stars,
            stars,
            (((1,), (1,)), ((), ())),
            precision=HIGHEST,
            preferred_element_type=jnp.float32,
        )
    )
    grams[me] = own_gram

    def gram_down(step, side, target, other_row):
        return pltpu.make_async_remote_copy(
            src_ref=grams.at[me],
            dst_ref=grams.at[me],
            send_sem=gram_send.at[step * rows_count + side],
            recv_sem=gram_recv.at[me],
            device_id=at(target, other_row),
            device_id_type=MESH,
        )

    def gram_up(target, other_row):
        return pltpu.make_async_remote_copy(
            src_ref=pair_sum,
            dst_ref=grams.at[me],
            send_sem=up_send.at[target * rows_count + other_row],
            recv_sem=gram_recv.at[me],
            device_id=at(target, other_row),
            device_id_type=MESH,
        )

    def gram_arrival(other_visit, other_row):
        other = other_visit * rows_count + other_row
        return pltpu.make_async_remote_copy(
            src_ref=grams.at[other],
            dst_ref=grams.at[other],
            send_sem=gram_send.at[0],
            recv_sem=gram_recv.at[other],
            device_id=at(other_visit, other_row),
            device_id_type=MESH,
        )

    pair_copy = gram_down(0, 0, visit, 1 - row)
    pair_copy.start()
    for step in range(1, visits):

        @pl.when(visit >= step)
        def _():
            gram_down(step, 0, visit - step, row).start()
            gram_down(step, 1, visit - step, 1 - row).start()

    @pl.loop(0, visit)
    def _(other):
        grams[other * rows_count] = jnp.zeros((8, TW), jnp.float32)

    for k in range(SLABS):
        padded[k, :, 0:PAD] = jnp.zeros((ROWS, PAD), jnp.bfloat16)
        padded[k, :, PAD + CW :] = jnp.zeros((ROWS, PAD), jnp.bfloat16)
    for step in range(visits):
        for k in range(SLABS):
            filled = OWN_K + k * HALO_K + NBASIS * HALO
            z[step, filled : OWN_K + (k + 1) * HALO_K, :] = jnp.zeros(
                (HALO_K - NBASIS * HALO, TILES_DEV * TW), jnp.bfloat16
            )
    for copy in small:
        copy.wait()
    tap = iota((NTAPS, 2 * TW), 0)
    lanes = iota((NTAPS, 2 * TW), 1)

    def spread(taps, here, index, there, other):
        one = jnp.where(lanes == jnp.bitwise_and(index, 2 * TW - 1), here, 0.0)
        two = jnp.where(lanes == jnp.bitwise_and(other, 2 * TW - 1), there, 0.0)
        return jnp.dot(taps, (one + two).astype(jnp.bfloat16), preferred_element_type=jnp.float32)

    reversed_taps = spread(column_tap_ref[...], 0.375, -tap, 0.625, -1 - tap)
    for b in range(NBASIS):
        base = jnp.broadcast_to(reversed_taps[b : b + 1, :], (2 * TW, 2 * TW))
        rolled = pltpu.roll(base, 0, 1, stride=1, stride_axis=0)
        band[:, b * TW : (b + 1) * TW] = rolled[:, 0:TW].astype(jnp.bfloat16)

    table = weight_ref[...].astype(jnp.float32)
    cell_visit, cell_ccd = iota(table.shape, 0), iota(table.shape, 1)

    def weight_of(source, k):
        hit = (cell_visit == source) & (cell_ccd == patch * C_DEV + k)
        return jnp.sum(jnp.where(hit, table, 0.0), keepdims=True)

    both = spread(row_tap_ref[...], 0.75, tap - HALF, 0.25, tap + 1 - HALF)
    alone = spread(row_tap_ref[...], 0.75, tap - HALF, 0.0, tap + 1 - HALF)
    lane = iota((R_DEV, TW), 1)
    wide_sub = iota((R_DEV, 2 * TW), 0)
    last = (wide_sub == R_DEV - 1) & (row == rows_count - 1)
    halo_parts = [jnp.zeros((R_DEV, TW), jnp.float32) for _ in range(HALO_K // TW)]
    for b in range(NBASIS):
        base = jnp.where(
            last,
            jnp.broadcast_to(alone[b : b + 1], (R_DEV, 2 * TW)),
            jnp.broadcast_to(both[b : b + 1], (R_DEV, 2 * TW)),
        )
        rolled = pltpu.roll(base, 0, 1, stride=1, stride_axis=0)
        plain[:, b * TW : (b + 1) * TW] = rolled[:, 0:TW]
        low = b % 8 * HALO
        piece = pltpu.roll(rolled[:, TW:], jnp.bitwise_and(low + row * HALO, TW - 1), 1)
        inside = (lane >= low) & (lane < low + HALO)
        halo_parts[b // 8] = jnp.where(inside, piece, halo_parts[b // 8])
    for t, part in enumerate(halo_parts):
        plain[:, (NBASIS + t) * TW : (NBASIS + t + 1) * TW] = part
    sets = iota(coeff_ref.shape, 1)
    for k in range(SLABS):
        picked = jnp.sum(
            jnp.where(sets == choice_ref[0, k], coeff_ref[...], 0.0), axis=1, keepdims=True
        )
        chosen[k] = jnp.broadcast_to(picked * weight_of(visit, k), (NBASIS, TW))

    def add_windows(index, owner):
        entries = []
        for e in range(CAP):
            q = owner * CAP + e
            k = list_ref[0, visit, 0, q]
            start = list_ref[1, visit, 0, q] + (PAD - HALF)
            tile = lax.shift_right_logical(start, 7)
            shift = start - tile * TW
            place = jnp.where(k >= 0, list_ref[2, visit, 0, q] * SLABS + k, -1)
            back = jnp.bitwise_and(TW - shift, TW - 1)
            entries.append((place, jnp.maximum(k, 0), tile, shift, back))
        selections = {unit: choose(entries, unit) for unit in (UNIT, HALO)}
        for first_row, unit in [(r, UNIT) for r in range(0, R_DEV, UNIT)] + [(R_DEV, HALO)]:
            spot = iota((unit, TW), 1)
            left, right = [], []
            for _, k, tile, shift, back in entries:
                parts = []
                for t in range(3):
                    at = (tile + t) * TW
                    piece = padded[k, first_row : first_row + unit, pl.ds(at, TW)]
                    parts.append(pltpu.roll(piece, back, 1))
                keep = spot < TW - shift
                left.append(jnp.where(keep, parts[0], parts[1]))
                right.append(jnp.where(keep, parts[1], parts[2]))
            windows = jnp.concatenate(
                [jnp.concatenate(left, axis=0), jnp.concatenate(right, axis=0)], axis=1
            )
            out = jnp.dot(selections[unit], windows, preferred_element_type=jnp.float32)
            out = out.astype(jnp.bfloat16)
            for p in range(PLACES):
                sums[index, p, first_row : first_row + unit, :] = out[p * unit : (p + 1) * unit]

    def filter_columns(index):
        block = sums[index].reshape(PLACES * ROWS, 2 * TW)
        out = jnp.dot(block, band[...], preferred_element_type=jnp.float32).astype(jnp.bfloat16)
        for p in range(PLACES):
            slot, k = p // SLABS, p % SLABS
            at = slice(slot * TW, (slot + 1) * TW)
            for b in range(NBASIS):
                m = k * NBASIS + b
                part = out[p * ROWS : (p + 1) * ROWS, b * TW : (b + 1) * TW]
                z[index, m * R_DEV : (m + 1) * R_DEV, at] = part[:R_DEV]
                halo_at = OWN_K + k * HALO_K + b * HALO
                z[index, halo_at : halo_at + HALO, at] = part[R_DEV:]

    for copy in loads:
        copy.wait()
    for copy in halo_copies:
        copy.wait_recv()

    def owner_of(step):
        if step == visits - 1:
            return visit
        if step == 0:
            return 1 - lax.div(visit + visits - 1, visits)
        odd = lax.rem(visit, 2)
        rising = step + lax.div(step + visits - visit, visits)
        falling = visits - step - lax.div(visit + step, visits)
        return odd * rising + (1 - odd) * falling

    gram_arrival(visit, 1 - row).wait_recv()
    pair_sum[...] = own_gram + grams[visit * rows_count + 1 - row]

    def prepare(step):
        add_windows(step, owner_of(step))
        filter_columns(step)

    for step in range(visits - 1):
        target = visit + step + 1

        @pl.when(target < visits)
        def _():
            pl.semaphore_wait(ready.at[target], 1 + row)

        @pl.when((target < visits) & (row == 1))
        def _():
            gram_up(target, 0).start()
            gram_up(target, 1).start()

        if step < BEFORE:
            prepare(step)

    for b in range(NBASIS):
        left, right = [], []
        for k in range(SLABS):
            wide = jnp.broadcast_to(chosen[k, b : b + 1], (R_DEV, TW))
            left.append((plain[:, b * TW : (b + 1) * TW] * wide).astype(jnp.bfloat16))
            m = k * NBASIS + b
            right.append(z[0, m * R_DEV : (m + 1) * R_DEV, :])
        products[b] = jnp.dot(
            jnp.concatenate(left, axis=1),
            jnp.concatenate(right, axis=0),
            preferred_element_type=jnp.float32,
        )

    for step in range(1, visits):

        @pl.when(visit >= step)
        def _():
            gram_arrival(visit - step, 1).wait_recv()

        @pl.when(visit + step < visits)
        def _():
            for r in range(rows_count):
                gram_arrival(visit + step, r).wait_recv()

    packed = grams[0]
    for s in range(1, members):
        packed = packed + grams[s]
    scales = basis_scales(packed)
    spot = iota((1, TW), 1)
    factors = [[scales[b][0:1] * chosen[k, b : b + 1] for b in range(NBASIS)] for k in range(SLABS)]
    for k in range(SLABS):
        for t in range(HALO_K // TW):
            along = jnp.zeros((1, TW), jnp.float32)
            for b in range(t * 8, min(t * 8 + 8, NBASIS)):
                along = jnp.where(spot >= b % 8 * HALO, factors[k][b], along)
            source = slice((NBASIS + t) * TW, (NBASIS + t + 1) * TW)
            target = OWN_K + k * HALO_K + t * TW
            wide = jnp.broadcast_to(along, (R_DEV, TW))
            mixed[:, target : target + TW] = (plain[:, source] * wide).astype(jnp.bfloat16)

    def scale_rows():
        for k in range(SLABS):
            for b in range(NBASIS):
                source, target = slice(b * TW, (b + 1) * TW), (k * NBASIS + b) * TW
                wide = jnp.broadcast_to(factors[k][b], (R_DEV, TW))
                mixed[:, target : target + TW] = (plain[:, source] * wide).astype(jnp.bfloat16)

    def put(out, owner):
        out = out.astype(jnp.bfloat16)
        for g in range(TILES_DEV):
            outgoing[owner, g] = out[:, g * TW : (g + 1) * TW]

    def mix_first(owner):
        out = jnp.dot(mixed[:, OWN_K:], z[0, OWN_K:, :], preferred_element_type=jnp.float32)
        for b in range(NBASIS):
            wide = jnp.broadcast_to(scales[b][0:1, 0:1], (R_DEV, TILES_DEV * TW))
            out = out + products[b] * wide
        put(out, owner)

    def mix_rows(index, owner):
        put(jnp.dot(mixed[...], z[index], preferred_element_type=jnp.float32), owner)

    tile_copies = []
    for step in range(visits - 1):
        owner = owner_of(step)
        if step == 0:
            mix_first(owner)
        else:
            if step == 1:
                scale_rows()
            if step >= BEFORE:
                prepare(step)
            mix_rows(step, owner)
        copy = pltpu.make_async_remote_copy(
            src_ref=outgoing.at[owner],
            dst_ref=incoming.at[visit],
            send_sem=tile_send.at[step],
            recv_sem=tile_recv.at[visit],
            device_id={"visit": owner},
            device_id_type=MESH,
        )
        copy.start()
        tile_copies.append(copy)
    prepare(visits - 1)
    mix_rows(visits - 1, visit)

    lower, inverse = factor_steps(unpack(packed))
    solved = jnp.dot(inverse, stars, precision=HIGHEST, preferred_element_type=jnp.float32)
    root = math.sqrt(star_total)
    factor_ref[0] = lower / root
    white_ref[0] = solved * root

    slot_lane = iota((1, list_vec.shape[3]), 1)
    mine = (slot_lane >= visit * CAP) & (slot_lane < visit * CAP + CAP)
    totals = [jnp.zeros((1, 1), jnp.float32) for _ in range(TILES_DEV)]
    for s in range(visits):
        block, slot = list_vec[0, s], list_vec[2, s]
        for g in range(TILES_DEV):
            for k in range(SLABS):
                ones = jnp.where(mine & (block == k) & (slot == g), 1.0, 0.0)
                count = jnp.sum(ones, axis=1, keepdims=True)
                totals[g] = totals[g] + count * weight_of(s, k)
    numerators = [outgoing[visit, g].astype(jnp.float32) for g in range(TILES_DEV)]
    for step in range(1, visits):
        source = lax.rem(visit + step, visits)
        pltpu.make_async_remote_copy(
            src_ref=outgoing.at[source],
            dst_ref=incoming.at[source],
            send_sem=tile_send.at[step - 1],
            recv_sem=tile_recv.at[source],
            device_id={"visit": source},
            device_id_type=MESH,
        ).wait_recv()
        for g in range(TILES_DEV):
            numerators[g] = numerators[g] + incoming[source, g].astype(jnp.float32)
    for g in range(TILES_DEV):
        coadd_ref[0, g] = numerators[g] / totals[g]
    for copy in halo_copies + [pair_copy] + tile_copies:
        copy.wait_send()
    for step in range(1, visits):

        @pl.when(visit >= step)
        def _():
            gram_down(step, 0, visit - step, row).wait_send()
            gram_down(step, 1, visit - step, 1 - row).wait_send()

        @pl.when((visit + step < visits) & (row == 1))
        def _():
            gram_up(visit + step, 0).wait_send()
            gram_up(visit + step, 1).wait_send()


def result_kernel(*refs):
    sources, targets, sem = refs[:3], refs[3:6], refs[6]
    copies = []
    for i, (source, target) in enumerate(zip(sources, targets)):
        copy = pltpu.make_async_copy(source, target, sem.at[i])
        copy.start()
        copies.append(copy)
    for copy in copies:
        copy.wait()


def on_device(
    exposures,
    kernel_choice,
    kernel_coeffs,
    row_taps,
    column_taps,
    visit_weight,
    footprints,
    star_coeffs,
):
    visits = lax.axis_size("visit")
    rows_count = lax.axis_size("row")
    members = visits * rows_count
    star_total = star_coeffs.shape[2] * members
    vmem = pl.BlockSpec(memory_space=pltpu.VMEM)
    anywhere = pl.BlockSpec(memory_space=pl.ANY)
    hbm = pl.BlockSpec(memory_space=pltpu.HBM)
    tiles = pltpu.VMEM((visits, TILES_DEV, R_DEV, TW), jnp.bfloat16)
    dma = pltpu.SemaphoreType.DMA
    operands = (
        kernel_choice,
        footprints,
        visit_weight,
        kernel_coeffs,
        row_taps,
        column_taps,
        star_coeffs,
        exposures,
    )
    results = pl.pallas_call(
        functools.partial(coadd_kernel, visits, rows_count, star_total),
        out_shape=(
            jax.ShapeDtypeStruct((1, TILES_DEV, R_DEV, TW), jnp.float32),
            jax.ShapeDtypeStruct((1, NCOMP, NCOMP), jnp.float32),
            jax.ShapeDtypeStruct(star_coeffs.shape, jnp.float32),
        ),
        in_specs=[hbm] * 8,
        out_specs=(vmem, vmem, vmem),
        scratch_shapes=[
            pltpu.SMEM(kernel_choice.shape, jnp.int32),
            pltpu.SMEM(footprints.shape, jnp.int32),
            pltpu.VMEM(footprints.shape, jnp.int32),
            pltpu.VMEM(visit_weight.shape, jnp.bfloat16),
            pltpu.VMEM(kernel_coeffs.shape, jnp.float32),
            pltpu.VMEM(row_taps.shape, jnp.bfloat16),
            pltpu.VMEM(column_taps.shape, jnp.bfloat16),
            pltpu.VMEM(star_coeffs.shape, jnp.float32),
            pltpu.VMEM((SLABS, ROWS, CW + 2 * PAD), jnp.bfloat16),
            pltpu.VMEM((visits, PLACES, ROWS, 2 * TW), jnp.bfloat16),
            pltpu.VMEM((2 * TW, NBASIS * TW), jnp.bfloat16),
            pltpu.VMEM((visits, ALL_K, TILES_DEV * TW), jnp.bfloat16),
            pltpu.VMEM((R_DEV, NBASIS * TW + HALO_K), jnp.float32),
            pltpu.VMEM((SLABS, NBASIS, TW), jnp.float32),
            pltpu.VMEM((NBASIS, R_DEV, TILES_DEV * TW), jnp.float32),
            pltpu.VMEM((R_DEV, ALL_K), jnp.bfloat16),
            pltpu.VMEM((members, 8, TW), jnp.float32),
            pltpu.VMEM((8, TW), jnp.float32),
            tiles,
            tiles,
            dma((7,)),
            dma,
            dma((SLABS,)),
            dma((SLABS,)),
            dma((SLABS,)),
            dma((members,)),
            dma((members,)),
            dma((members,)),
            pltpu.SemaphoreType.REGULAR((visits,)),
            dma((visits,)),
            dma((visits,)),
        ],
        compiler_params=pltpu.CompilerParams(
            vmem_limit_bytes=VMEM_LIMIT, collective_id=0, has_side_effects=True
        ),
        name="coadd",
    )(*[pltpu.with_memory_space_constraint(x, pltpu.HBM) for x in operands])
    return pl.pallas_call(
        result_kernel,
        out_shape=tuple(jax.ShapeDtypeStruct(part.shape, part.dtype) for part in results),
        in_specs=[anywhere] * 3,
        out_specs=(anywhere,) * 3,
        scratch_shapes=[dma((3,))],
        compiler_params=pltpu.CompilerParams(vmem_limit_bytes=4 * 1024 * 1024),
        name="results",
    )(*results)


def solution(mesh):
    in_specs = (
        P(("blk", "visit"), "patch", "row", None),
        P(("blk", "visit"), "patch"),
        P(),
        P(),
        P(),
        P("blk", None),
        P(None, "blk", "patch", None),
        P(("blk", "patch"), None, ("visit", "row")),
    )
    out_specs = (
        P(("blk", "patch"), "visit", "row", None),
        P(("blk", "patch"), None, None),
        P(("blk", "patch"), None, ("visit", "row")),
    )
    return jax.shard_map(
        on_device, mesh=mesh, in_specs=in_specs, out_specs=out_specs, check_vma=False
    )
```
